32 devices in a mesh: pipe: 4 (over y, core), ctx: 8 (over z, x).
Axes of the slice: x: 2, y: 2, z: 4, core: 2. Of those that a mesh axis runs over, the one named last changes fastest.
Arguments:
- x_proj: bfloat16 [4, 2, 1024, 2048], P('pipe', None, 'ctx'), may hold values from -6 to 6
- gate_proj: bfloat16 [4, 2, 1024, 2048], P('pipe', None, 'ctx'), may hold values from -6 to 6
- bc_proj: bfloat16 [4, 2, 1024, 1024], P('pipe', None, 'ctx'), may hold values from -6 to 6
- dt_raw: float32 [4, 2, 1024, 64], P('pipe', None, 'ctx'), may hold values from -3 to 16
- decay_rate: float32 [4, 64], P('pipe'), may hold values from 0 to 1
- conv_weight: float32 [4, 4, 3072], P('pipe'), may hold values from -3 to 3
- skip_gain: float32 [4, 64], P('pipe'), may hold values from 0.5 to 1.5
- norm_gain: float32 [4, 2048], P('pipe'), may hold values from 0.1 to 1.9
Outputs:
- mixed_out: bfloat16 [4, 2, 1024, 2048], P('pipe', None, 'ctx')
The draws below stay inside these ranges and needn't reach their ends.
All inputs are finite; a program needn't handle non-finite values.
Results may differ from the reference program's by a relative error of at most 0.0052.
Values may be sent and summed in bfloat16 or wider, within the bound.
A program may use at most 64 MiB of HBM per device.

```python
import math
import jax
import jax.numpy as jnp
from jax import lax

HEADS = 64
HEAD_DIM = 32
GROUPS = 8
STATE = 64
KERNEL = 4
BLOCK = 128
SEQS = 2
LAYERS = 4
SEQUENCE_TOKENS = 1024
HD = 2048
CH = 3072


def draw_dt_raw(key, part):
    random_key_root, random_key_position, random_key_range = jax.random.split(key, 3)
    tensor_dimensions = (LAYERS, SEQS, SEQUENCE_TOKENS, HEADS)
    baseline_result = jnp.clip(0.5 * jax.random.normal(random_key_root, tensor_dimensions, jnp.float32), -3.0, 3.0)
    range_positions = jax.random.randint(random_key_position, (LAYERS, SEQS, 3), 0, SEQUENCE_TOKENS)
    range_token_rows = jnp.any(jnp.arange(SEQUENCE_TOKENS)[None, None, :, None] == range_positions[:, :, None, :], axis=-1)
    token_ranges = jax.random.uniform(random_key_range, tensor_dimensions, jnp.float32, 8.0, 16.0)
    return jnp.where(range_token_rows[..., None], token_ranges, baseline_result)


def draw_decay_rate(key, part):
    fraction = jax.random.uniform(key, (LAYERS, HEADS), jnp.float32)
    low_end = math.log(0.2 / SEQUENCE_TOKENS)
    high_end = math.log(60.0 / SEQUENCE_TOKENS)
    return jnp.exp(low_end + fraction * (high_end - low_end))


def levels(key, extent, pieces, least, high):
    factor_of = 1.0
    for axis_at, blocks in pieces:
        heights = jax.random.uniform(jax.random.fold_in(jax.random.fold_in(key, 6), axis_at), (blocks,), jnp.float32, least / len(pieces), high / len(pieces))
        factor_of = factor_of * jnp.repeat(jnp.exp(heights), extent[axis_at] // blocks).reshape((-1,) + (1,) * (len(extent) - 1 - axis_at))
    return factor_of


def centred(rng, shape, width, bound, cuts=(), held_as=jnp.bfloat16):
    drawn = width * jax.random.normal(rng, shape, jnp.float32)
    if cuts:
        drawn = drawn * levels(rng, shape, cuts, -0.22, 0.18)
    return jnp.clip(drawn, -bound, bound).astype(held_as)


def setup_inputs(seed: int = 0) -> dict:
    key_of = jax.random.split(jax.random.key(seed), 9)
    return {
        "x_proj": centred(key_of[0], (LAYERS, SEQS, SEQUENCE_TOKENS, HD), 1.0, 6.0, ((0, 4), (2, 8))),
        "gate_proj": centred(key_of[1], (LAYERS, SEQS, SEQUENCE_TOKENS, HD), 1.0, 6.0, ((0, 4), (2, 8))),
        "bc_proj": centred(key_of[2], (LAYERS, SEQS, SEQUENCE_TOKENS, 2 * GROUPS * STATE), 1.0, 6.0, ((0, 4), (2, 8))),
        "dt_raw": draw_dt_raw(jax.random.fold_in(key_of[8], 71), 0),
        "decay_rate": draw_decay_rate(jax.random.fold_in(key_of[8], 71), 0),
        "conv_weight": centred(key_of[5], (LAYERS, KERNEL, CH), KERNEL ** -0.5, 3.0, ((0, 4),), jnp.float32),
        "skip_gain": jnp.clip(0.5 + 1.0 * jax.random.uniform(key_of[6], (LAYERS, HEADS), jnp.float32) ** levels(key_of[6], (LAYERS, HEADS), ((0, 4),), -0.2, 0.2), 0.5, 1.5),
        "norm_gain": jnp.clip(1.0 + 0.18 * jax.random.normal(key_of[7], (LAYERS, HD), jnp.float32), 0.1, 1.9),
    }


norm_eps = 1e-05
precise_mode = lax.Precision.HIGHEST

def rounded(value):
    return lax.optimization_barrier(value.astype(jnp.bfloat16)).astype(jnp.float32)

def convolve(inputs, weight, head_rows):
    tap_count = weight.shape[0]
    padded = jnp.concatenate([head_rows, inputs], axis=0)
    length = inputs.shape[0]
    conv_sum = weight[0] * padded[0:length]
    for offset in range(1, tap_count):
        conv_sum = conv_sum + weight[offset] * padded[offset:offset + length]
    return jax.nn.silu(conv_sum)

def block_terms(activated, dt_rows, rates):
    feature_width = HEADS * HEAD_DIM
    bc_width = GROUPS * STATE
    per_group = HEADS // GROUPS
    block_count = activated.shape[0] // BLOCK
    inputs_x = activated[:, :feature_width].reshape(block_count, BLOCK, HEADS, HEAD_DIM)
    inputs_b = activated[:, feature_width:feature_width + bc_width].reshape(block_count, BLOCK, GROUPS, STATE)
    inputs_c = activated[:, feature_width + bc_width:].reshape(block_count, BLOCK, GROUPS, STATE)
    steps_dt = jax.nn.softplus(dt_rows).reshape(block_count, BLOCK, HEADS)
    cumulated = jnp.cumsum(-steps_dt * rates, axis=1)
    scores = jnp.einsum('cign,cjgn->cgij', inputs_c, inputs_b, precision=precise_mode)
    scores = jnp.repeat(scores, per_group, axis=1)
    cumul_heads = jnp.transpose(cumulated, (0, 2, 1))
    lower_mask = jnp.arange(BLOCK)[:, None] >= jnp.arange(BLOCK)[None, :]
    log_gaps = cumul_heads[:, :, :, None] - cumul_heads[:, :, None, :]
    decays = jnp.where(lower_mask, jnp.exp(jnp.where(lower_mask, log_gaps, 0.0)), 0.0)
    dt_heads = jnp.transpose(steps_dt, (0, 2, 1))
    weights = rounded(scores * decays * dt_heads[:, :, None, :])
    diag_out = jnp.einsum('chij,cjhp->cihp', weights, inputs_x, precision=precise_mode)
    block_ends = cumulated[:, -1, :]
    tail_weight = jnp.exp(block_ends[:, None, :] - cumulated) * steps_dt
    keyed_rows = rounded(jnp.repeat(inputs_b, per_group, axis=2) * tail_weight[..., None])
    local_states = jnp.einsum('cqhn,cqhp->chpn', keyed_rows, inputs_x, precision=precise_mode)
    return (inputs_x, inputs_c, cumulated, diag_out, local_states, jnp.exp(block_ends))

def finish(inputs_x, inputs_c, cumulated, diag_out, incoming, skips, gate_rows, gains):
    per_group = HEADS // GROUPS
    state_rows = rounded(incoming)
    off_out = jnp.einsum('cqhn,chpn->cqhp', jnp.repeat(inputs_c, per_group, axis=2), state_rows, precision=precise_mode)
    off_out = off_out * jnp.exp(cumulated)[..., None]
    mixed_sum = diag_out + off_out + skips[None, None, :, None] * inputs_x
    length = mixed_sum.shape[0] * mixed_sum.shape[1]
    feature_width = HEADS * HEAD_DIM
    gated_rows = mixed_sum.reshape(length, feature_width) * jax.nn.silu(gate_rows.astype(jnp.float32))
    grouped = gated_rows.reshape(length, GROUPS, feature_width // GROUPS)
    inv_rms = lax.rsqrt(lax.optimization_barrier(jnp.mean(grouped * grouped, axis=-1, keepdims=True)) + norm_eps)
    return ((grouped * inv_rms).reshape(length, feature_width) * gains).astype(jnp.bfloat16)

def sequence_out(x_rows, prev_rows, bc_rows, dt_rows, gate_rows, rates, weight, skips, gains):
    conv_in = jnp.concatenate([x_rows.astype(jnp.float32) + prev_rows.astype(jnp.float32), bc_rows.astype(jnp.float32)], axis=1)
    head_rows = jnp.zeros((weight.shape[0] - 1, conv_in.shape[1]), jnp.float32)
    activated = rounded(convolve(conv_in, weight, head_rows))
    inputs_x, inputs_c, cumulated, diag_out, local_states, factors = block_terms(activated, dt_rows, rates)

    def advance(held_state, step_pair):
        factor, own_term = step_pair
        return (factor[:, None, None] * held_state + own_term, held_state)
    zero_state = jnp.zeros((HEADS, HEAD_DIM, STATE), jnp.float32)
    final_state, incoming = lax.scan(advance, zero_state, (factors, local_states))
    return finish(inputs_x, inputs_c, cumulated, diag_out, incoming, skips, gate_rows, gains)

def reference(x_proj, gate_proj, bc_proj, dt_raw, decay_rate, conv_weight, skip_gain, norm_gain):
    previous = jnp.zeros((SEQS, SEQUENCE_TOKENS, HEADS * HEAD_DIM), jnp.bfloat16)
    outputs = []
    for layer_idx in range(LAYERS):

        def one_sequence(seq_index, layer_idx=layer_idx, previous=previous):
            return sequence_out(x_proj[layer_idx, seq_index], previous[seq_index], bc_proj[layer_idx, seq_index], dt_raw[layer_idx, seq_index], gate_proj[layer_idx, seq_index], decay_rate[layer_idx], conv_weight[layer_idx], skip_gain[layer_idx], norm_gain[layer_idx])
        previous = lax.map(one_sequence, jnp.arange(SEQS))
        outputs.append(previous)
    return jnp.stack(outputs, axis=0)
```

```python
import functools

import jax
import jax.numpy as jnp
from jax import lax
from jax.experimental import pallas as pl
from jax.experimental.pallas import tpu as pltpu
from jax.sharding import PartitionSpec as P

HEADS = 64
HEAD_DIM = 32
GROUPS = 8
STATE = 64
BLOCK = 128
HALF = BLOCK // 2
SEQS = 2
PER_GROUP = HEADS // GROUPS
WIDTH = PER_GROUP * HEAD_DIM
HD = HEADS * HEAD_DIM
UNITS = SEQS * GROUPS
PAIRS = UNITS // 2
EDGE = 16
PAD = 8
KEPT = 4
FOLD = (HD + 2 * GROUPS * STATE) * KEPT // EDGE
TAPS = 4
FEW = 6
EVEN = 8
ROWS = 2 * BLOCK + EDGE

norm_eps = 1e-05
MESH = pl.DeviceIdType.MESH
HIGHEST = lax.Precision.HIGHEST
LOG2E = 1.4426950408889634


def silu_of_twice(half):
    return half * jnp.tanh(half) + half


def conv(buf, weight):
    first = PAD - TAPS + 1
    halves = 0.5 * weight
    total = halves[0:1] * buf[first : first + BLOCK]
    for tap in range(1, TAPS):
        total = total + halves[tap : tap + 1] * buf[first + tap : first + tap + BLOCK]
    return silu_of_twice(total)


def pieces(v):
    parts = []
    for _ in range(3):
        part = v.astype(jnp.bfloat16).astype(jnp.float32)
        parts.append(part)
        v = v - part
    return parts


def kernel(
    stages,
    ranges,
    x_hbm,
    gate_hbm,
    bc_hbm,
    dt_hbm,
    rate_hbm,
    w_hbm,
    skip_hbm,
    gain_hbm,
    out_ref,
    dt_ref,
    rate_ref,
    skip_ref,
    w_buf,
    gain_buf,
    x_buf,
    gate_buf,
    bc_buf,
    lead_buf,
    key_buf,
    pair_buf,
    keys,
    chosen,
    masked,
    shifted,
    weights,
    b_rows,
    c_rows,
    wides,
    tails,
    cbuf,
    bbuf,
    head_out,
    head_in,
    heads,
    flow,
    edge,
    edge_out,
    state_in,
    state_out,
    fetch_sem,
    part_send,
    part_recv,
    swap_send,
    swap_recv,
    head_send,
    head_recv,
    prev_send,
    prev_recv,
    edge_send,
    edge_recv,
    state_send,
    state_recv,
    out_send,
    out_recv,
):
    f32, bf16 = jnp.float32, jnp.bfloat16
    section = lax.axis_index("pipe")
    mine = lax.axis_index("ctx")
    stage, core = section // 2, section % 2
    other = 2 * stage + 1 - core
    has_down = stage < stages - 1
    has_up = stage > 0
    has_right = mine < ranges - 1
    has_left = mine > 0
    first_chip = (stage == 0) & (mine == 0)

    def share(at_stage, at_range):
        return jnp.maximum(FEW, EVEN - (EVEN - FEW) * (at_range // 2 + at_stage))

    def owner(u, at_stage, at_range):
        return 2 * at_stage + (u >= share(at_stage, at_range)).astype(jnp.int32)

    shared = share(stage, mine)
    low = core * shared
    many = shared + core * (UNITS - 2 * shared)
    first_pair, n_pairs = low // 2, many // 2
    far_pair, far_pairs = (1 - core) * (shared // 2), PAIRS - n_pairs

    fetches = [
        pltpu.make_async_copy(src, dst, fetch_sem.at[i])
        for i, (src, dst) in enumerate(
            (
                (dt_hbm, dt_ref),
                (rate_hbm, rate_ref),
                (skip_hbm, skip_ref),
                (bc_hbm.at[0], bc_buf.at[core]),
                (x_hbm.at[0], x_buf.at[core]),
                (w_hbm.at[0], w_buf.at[core]),
                (gain_hbm, gain_buf.at[core]),
                (gate_hbm.at[0], gate_buf.at[core]),
            )
        )
    ]
    for fetch in fetches:
        fetch.start()

    barrier = pltpu.get_barrier_semaphore()
    partners = [(core >= 0, other, 0)]
    for there, down, along in (
        (has_right, 0, 1),
        (has_left, 0, -1),
        (has_down, 1, 0),
        (has_up, -1, 0),
        (has_down & has_right, 1, 1),
        (has_up & has_left, -1, -1),
    ):
        for side in range(2):
            partners.append((there, 2 * (stage + down) + side, along))
    count = 0
    for there, to, along in partners:
        count = count + there.astype(jnp.int32)

        @pl.when(there)
        def _(to=to, along=along):
            pl.semaphore_signal(
                barrier,
                inc=1,
                device_id={"pipe": to, "ctx": mine + along},
                device_id_type=MESH,
            )

    def remote(src, dst, send, recv, to, along=0):
        return pltpu.make_async_remote_copy(
            src_ref=src,
            dst_ref=dst,
            send_sem=send,
            recv_sem=recv,
            device_id={"pipe": to, "ctx": mine + along},
            device_id_type=MESH,
        )

    def part_copy(i, k):
        src, dst = (
            (lead_buf.at[k], lead_buf),
            (key_buf.at[k], key_buf),
            (pair_buf.at[k], pair_buf),
            (w_hbm.at[0], w_buf),
            (gain_hbm, gain_buf),
        )[i]
        return remote(src, dst.at[k], part_send.at[i], part_recv.at[i], other)

    def swap_copy(kind, k, p):
        s, at = p // (GROUPS // 2), p % (GROUPS // 2)
        if kind < 2:
            lanes = pl.ds(pl.multiple_of(kind * GROUPS * STATE + at * 2 * STATE, 2 * STATE), 2 * STATE)
            src, dst = bc_hbm, bc_buf
        else:
            lanes = pl.ds(pl.multiple_of(at * 2 * WIDTH, 2 * WIDTH), 2 * WIDTH)
            src, dst = ((x_hbm, x_buf), (gate_hbm, gate_buf))[kind - 2]
        return remote(
            src.at[0, s, :, lanes],
            dst.at[k, s, :, lanes],
            swap_send.at[kind // 2],
            swap_recv.at[kind // 2, p],
            other,
        )

    def swap_wait(half, k, p):
        ref = (bc_buf.at[k, 0, :, pl.ds(0, 4 * STATE)], x_buf.at[k, 0, :, pl.ds(0, 4 * WIDTH)])[half]
        remote(ref, ref, swap_send.at[half], swap_recv.at[half, p], other).wait_recv()

    HEAD_PARTS = ((0, 0), (0, 1), (1, 1))

    def head_copy(k, i):
        s, side = HEAD_PARTS[i]
        return remote(
            head_out.at[s],
            head_in.at[k, s],
            head_send.at[i],
            head_recv.at[k, s],
            2 * stage + side,
            1,
        )

    def prev_copy(p):
        both = pl.ds(2 * p, 2)
        return remote(
            flow.at[2, both], flow.at[0, both], prev_send, prev_recv.at[p], owner(2 * p, stage + 1, mine)
        )

    def edge_copy(k, p):
        both = pl.ds(2 * p, 2)
        return remote(
            edge_out.at[k, both],
            edge.at[k, both],
            edge_send.at[k],
            edge_recv.at[k, p],
            owner(2 * p, stage + 1 - k, mine + 1),
            1,
        )

    def state_copy(k, u):
        return remote(
            state_out.at[k, u],
            state_in.at[k, u],
            state_send,
            state_recv.at[k, u],
            owner(u, stage, mine + 1),
            1,
        )

    def out_copy(k, u):
        lanes = pl.ds(pl.multiple_of((u % GROUPS) * WIDTH, WIDTH), WIDTH)
        return remote(
            flow.at[k + 1, u],
            out_ref.at[0, u // GROUPS, :, lanes],
            out_send,
            out_recv,
            other,
        )

    sh_rows = lax.broadcasted_iota(jnp.int32, (2 * BLOCK, 2 * WIDTH), 0)
    sh_cols = lax.broadcasted_iota(jnp.int32, (2 * BLOCK, 2 * WIDTH), 1)
    shifted[...] = (sh_rows == BLOCK + sh_cols // HEAD_DIM).astype(bf16)
    ch_rows = lax.broadcasted_iota(jnp.int32, (3 * 32, PER_GROUP * HALF), 0)
    ch_cols = lax.broadcasted_iota(jnp.int32, (3 * 32, PER_GROUP * HALF), 1)
    chosen[...] = (ch_rows % PER_GROUP == ch_cols // HALF).astype(bf16)
    masked[...] = jnp.where(ch_rows[:HALF] < ch_cols[:HALF] % HALF, -1e30, 0.0).astype(bf16)

    for fetch in fetches[:3]:
        fetch.wait()
    rows = lax.broadcasted_iota(jnp.int32, (BLOCK, BLOCK), 0)
    cols = lax.broadcasted_iota(jnp.int32, (BLOCK, BLOCK), 1)
    raw = jnp.concatenate([dt_ref[0, s] for s in range(SEQS)], axis=0)
    steps = jnp.maximum(raw, 0.0) + jnp.log1p(jnp.exp(-jnp.abs(raw)))
    rates = jnp.concatenate([rate_ref[...]] * SEQS, axis=1)
    rates = jnp.broadcast_to(rates, (BLOCK, SEQS * HEADS)).T
    summed = jnp.dot(
        -steps * rates,
        (rows <= cols).astype(f32),
        precision=HIGHEST,
        preferred_element_type=f32,
    )
    keys[...] = summed * LOG2E - jnp.log2(steps)
    left = cols < HALF
    one_keys, two_keys = [], []
    for q in range(PER_GROUP // 2):
        one = keys[pl.ds(2 * q, UNITS, stride=PER_GROUP), :]
        two = keys[pl.ds(2 * q + 1, UNITS, stride=PER_GROUP), :]
        one_keys.append(jnp.where(left[:UNITS], one, pltpu.roll(two, HALF, 1)))
        two_keys.append(jnp.where(left[:UNITS], pltpu.roll(one, HALF, 1), two))
    stacked = jnp.concatenate(
        pieces(jnp.concatenate(one_keys, axis=1)) + pieces(jnp.concatenate(two_keys, axis=1)), axis=0
    ).astype(bf16)
    order = ((cols // UNITS == rows % PER_GROUP) & (cols % UNITS == rows // PER_GROUP))[:, : 6 * UNITS]
    key_buf[core] = jnp.dot(
        order.astype(bf16), stacked, preferred_element_type=f32
    ).astype(bf16)
    cum = summed.T
    slot = cols % PER_GROUP
    halves = jnp.where((slot < 6) & (slot // 3 == rows // HALF), -1.0, 0.0)
    leads = pieces(cum * LOG2E)
    for quad in range(UNITS // 4):
        lead = halves
        for i in (2, 1, 0):
            turn = (32 * (i - quad)) % BLOCK
            part = pltpu.roll(leads[i], turn, 1) if turn else leads[i]
            lead = jnp.where(cols < 32 * (i + 1), part, lead)
        lead_buf[core, quad] = lead.astype(bf16)
    middle, end = cum[HALF - 1 : HALF], cum[BLOCK - 1 : BLOCK]
    grown = jnp.exp(jnp.where(rows < HALF, cum, cum - middle))
    tail = jnp.exp(jnp.where(rows < HALF, middle, end) - cum) * steps.T
    skips = jnp.concatenate([skip_ref[...]] * SEQS, axis=1)
    extra = jnp.zeros((EDGE, BLOCK), f32)
    slot = rows[:EDGE]
    for i, row in enumerate((skips, grown[HALF - 1 : HALF], grown[BLOCK - 1 : BLOCK])):
        row_high = row.astype(bf16).astype(f32)
        extra = jnp.where(slot == 2 * i, row_high, extra)
        extra = jnp.where(slot == 2 * i + 1, row - row_high, extra)
    pair_buf[core] = jnp.concatenate([grown, extra, tail], axis=0).astype(bf16)

    fetches[3].wait()
    fetches[4].wait()
    for s in range(SEQS):
        last = jnp.concatenate(
            [
                ref[core, s, BLOCK - EDGE :, :].astype(f32)[EDGE - KEPT :]
                for ref in (x_buf, bc_buf)
            ],
            axis=1,
        )
        head_out[s] = jnp.concatenate(
            [last[:, m * FOLD : (m + 1) * FOLD] for m in range(EDGE // KEPT)], axis=0
        ).astype(bf16)
    pl.semaphore_wait(barrier, count)

    @pl.when(has_right)
    def _():
        for i in range(3):
            head_copy(core, i).start()

    for i in range(4):
        part_copy(i, core).start()

    def swap(p, carry):
        for kind in range(4):
            swap_copy(kind, core, p).start()
        return carry

    lax.fori_loop(far_pair, far_pair + far_pairs, swap, 0)
    part_copy(4, core).start()

    @pl.when(jnp.logical_not(has_left))
    def _():
        heads[...] = jnp.zeros_like(heads)

    @pl.when(has_left)
    def _():
        def unfold(k, s):
            folded = head_in[k, s].astype(f32)
            for m in range(EDGE // KEPT):
                heads[k, s * PAD + PAD - KEPT : (s + 1) * PAD, m * FOLD : (m + 1) * FOLD] = folded[
                    m * KEPT : (m + 1) * KEPT
                ]

        for k in range(2):
            head_copy(k, 0).wait_recv()
            unfold(k, 0)

            @pl.when(core == 1)
            def _(k=k):
                head_copy(k, 2).wait_recv()
                unfold(k, 1)

    fetches[5].wait()
    left = left[:HALF]
    unit_of = cols % 32 // PER_GROUP
    token_of = (rows % HALF == cols)[:, :HALF].astype(bf16)

    def prepare(k, p):
        @pl.when(k != core)
        def _():
            @pl.when(p == first_pair)
            def _():
                for i in range(5):
                    part_copy(i, k).wait_recv()

            swap_wait(0, k, p)

        s, pair = p // (GROUPS // 2), p % (GROUPS // 2)
        acts = []
        for part in range(2):
            at = pl.multiple_of(part * GROUPS * STATE + pair * 2 * STATE, 2 * STATE)
            wide = pl.ds(pl.multiple_of(HD + at, 2 * STATE), 2 * STATE)
            bbuf[part, pl.ds(0, PAD), :] = heads[k, pl.ds(pl.multiple_of(s * PAD, PAD), PAD), wide]
            bbuf[part, pl.ds(PAD, BLOCK), :] = bc_buf[k, s, :, pl.ds(at, 2 * STATE)].astype(f32)
            acts.append(conv(bbuf.at[part], w_buf[k, :, wide]).astype(bf16))
        b_t = acts[0].astype(f32).T
        quad = p // 2
        lead = lead_buf[k, quad]
        chooser = jnp.concatenate(
            [chosen[...], key_buf[k, pl.ds(pl.multiple_of(quad * 32, 32), 32), :], masked[...]], axis=0
        )
        lead_rows = [
            jnp.where(unit_of == (2 * p + half) % 4, lead, jnp.zeros_like(lead)) for half in range(2)
        ]
        gap = jnp.dot(
            jnp.concatenate(
                [jnp.concatenate(lead_rows, axis=0), jnp.concatenate([token_of] * 2, axis=0)], axis=1
            ),
            chooser,
            preferred_element_type=f32,
        )
        spread = shifted[pl.ds(pl.multiple_of(BLOCK - 2 * PER_GROUP * p, 2 * PER_GROUP), BLOCK), :]
        wide = jnp.dot(pair_buf[k], spread, preferred_element_type=f32)
        for half in range(2):
            u = 2 * p + half
            c_u = acts[1][:, half * STATE : (half + 1) * STATE]
            b_u = b_t[half * STATE : (half + 1) * STATE]
            b_turned = pltpu.roll(b_u, HALF, 1)
            b_one = jnp.where(left, b_u, b_turned).astype(bf16)
            b_two = jnp.where(left, b_turned, b_u).astype(bf16)
            c_rows[k, u] = c_u
            b_rows[k, u, 0] = b_one[:, :HALF]
            b_rows[k, u, 1] = b_two[:, :HALF]
            scores = (
                jnp.dot(c_u[:HALF], b_one, preferred_element_type=f32),
                jnp.dot(c_u[HALF:], b_two, preferred_element_type=f32),
            )
            for part in range(2):
                tokens = slice(part * HALF, (part + 1) * HALF)
                gap_rows = slice((2 * half + part) * HALF, (2 * half + part + 1) * HALF)
                for q in range(PER_GROUP // 2):
                    lanes = slice(q * BLOCK, (q + 1) * BLOCK)
                    weights[k, u, tokens, lanes] = (
                        scores[part] * jnp.exp2(gap[gap_rows, lanes])
                    ).astype(bf16)
            here = slice(half * WIDTH, (half + 1) * WIDTH)
            wides[k, u] = wide[: BLOCK + EDGE, here]
            tails[k, u] = wide[BLOCK + EDGE :, here].astype(bf16)

    def ahead(i, carry):
        turn = i // n_pairs
        k = core + turn * (1 - 2 * core)
        prepare(k, first_pair + i % n_pairs)
        return carry

    lazy = first_chip.astype(jnp.int32)
    lax.fori_loop(0, n_pairs * (2 - lazy - lazy * (1 - core)), ahead, 0)

    fetches[6].wait()
    fetches[7].wait()
    lane_head = lax.broadcasted_iota(jnp.int32, (HALF, BLOCK), 1) // HEAD_DIM

    def work(k, p):
        s = p // (GROUPS // 2)
        both = (2 * p, 2 * p + 1)

        def lanes_of(u, side=0, width=WIDTH):
            return pl.ds(pl.multiple_of((u % GROUPS) * WIDTH + side * width, width), width)

        @pl.when((k == 0) & has_up)
        def _():
            prev_copy(p).wait_recv()

        @pl.when(has_left & ((k == 1) | has_up))
        def _():
            edge_copy(k, p).wait_recv()

        @pl.when((k == 0) & jnp.logical_not(has_up))
        def _():
            for u in both:
                flow[0, u] = jnp.zeros(flow.shape[2:], bf16)

        @pl.when(jnp.logical_not(has_left & ((k == 1) | has_up)))
        def _():
            for u in both:
                edge[k, u] = jnp.zeros(edge.shape[2:], f32)

        @pl.when(jnp.logical_not(has_left))
        def _():
            for u in both:
                state_in[k, u] = jnp.zeros(state_in.shape[2:], bf16)

        xs_of, falls, locals_one, locals_all, mixed_of = [], [], [], [], []
        for i, u in enumerate(both):
            sides = []
            for side in range(2):
                at = lanes_of(u, side, BLOCK)
                buf = cbuf.at[2 * i + side]
                buf[pl.ds(0, PAD), :] = heads[k, pl.ds(pl.multiple_of(s * PAD, PAD), PAD), at]
                buf[pl.ds(PAD - KEPT, KEPT), :] += edge[k, u, side * KEPT : (side + 1) * KEPT]
                buf[pl.ds(PAD, BLOCK), :] = x_buf[k, s, :, at].astype(f32) + flow[
                    k, u, :, side * BLOCK : (side + 1) * BLOCK
                ].astype(f32)
                sides.append(conv(buf, w_buf[k, :, at]).astype(bf16))
            xs = jnp.concatenate(sides, axis=1)
            xs_of.append(xs)
            keyed = xs * tails[k, u]
            extra = wides[k, u, BLOCK : BLOCK + PAD]
            fall_one, fall_two = extra[2:3] + extra[3:4], extra[4:5] + extra[5:6]
            local_one = jnp.dot(b_rows[k, u, 0], keyed[:HALF], preferred_element_type=f32)
            local_two = jnp.dot(b_rows[k, u, 1], keyed[HALF:], preferred_element_type=f32)
            falls.append((fall_one, fall_two))
            locals_one.append(local_one)
            locals_all.append(fall_two * local_one + local_two)
        zero = jnp.zeros((HALF, BLOCK), bf16)
        for u, xs in zip(both, xs_of):
            mixed = []
            for part in range(2):
                tokens = slice(part * HALF, (part + 1) * HALF)
                sides = []
                for side in range(2):
                    xs_side = xs[tokens, side * BLOCK : (side + 1) * BLOCK]
                    diagonal = jnp.concatenate(
                        [jnp.where(lane_head == h, xs_side, zero) for h in range(PER_GROUP // 2)],
                        axis=0,
                    )
                    sides.append(
                        jnp.dot(
                            weights[k, u, tokens, side * WIDTH : (side + 1) * WIDTH],
                            diagonal,
                            preferred_element_type=f32,
                        )
                    )
                mixed.append(jnp.concatenate(sides, axis=1))
            skip = wides[k, u, BLOCK : BLOCK + 1] + wides[k, u, BLOCK + 1 : BLOCK + 2]
            mixed_of.append(jnp.concatenate(mixed, axis=0) + skip * xs.astype(f32))

        arrived = []
        for i, u in enumerate(both):

            @pl.when(has_left)
            def _(u=u):
                state_copy(k, u).wait_recv()

            incoming = state_in[k, u].astype(f32)
            fall_one, fall_two = falls[i]
            state_out[k, u] = ((fall_one * fall_two) * incoming + locals_all[i]).astype(bf16)
            arrived.append(incoming)

            @pl.when(has_right)
            def _(u=u):
                state_copy(k, u).start()

        for i, u in enumerate(both):
            incoming = arrived[i]
            between = (falls[i][0] * incoming + locals_one[i]).astype(bf16)
            off = jnp.concatenate(
                [
                    jnp.dot(c_rows[k, u, :HALF], incoming.astype(bf16), preferred_element_type=f32),
                    jnp.dot(c_rows[k, u, HALF:], between, preferred_element_type=f32),
                ],
                axis=0,
            )
            mixed = mixed_of[i] + off * wides[k, u, :BLOCK]
            gate = (0.5 * gate_buf[k, s, :, lanes_of(u)]).astype(f32)
            gated = mixed * silu_of_twice(gate)
            mean = jnp.sum(gated * gated, axis=1, keepdims=True) * (1.0 / WIDTH)
            result = (
                gated * lax.rsqrt(mean + norm_eps) * gain_buf[k, 0:1, lanes_of(u)]
            ).astype(bf16)
            flow[k + 1, u] = result
            last = result[BLOCK - EDGE :].astype(f32)[EDGE - KEPT :]
            edge_out[1 - k, u] = jnp.concatenate([last[:, :BLOCK], last[:, BLOCK:]], axis=0)

        @pl.when(has_right & ((k == 0) | has_down))
        def _():
            edge_copy(1 - k, p).start()

        @pl.when((k == 1) & has_down)
        def _():
            prev_copy(p).start()

        @pl.when(k == core)
        def _():
            for u in both:
                out_ref[0, s, :, lanes_of(u)] = flow[k + 1, u]

        @pl.when(k != core)
        def _():
            for u in both:
                out_copy(k, u).start()

    few, even = FEW // 2, EVEN // 2

    def step(i, carry):
        k, i = i % 2, i // 2
        later = jnp.maximum(i - few, 0)
        p = jnp.where(
            core == 0,
            i,
            jnp.where(i < few, even + i, few + later // 2 + even * (later % 2)),
        )

        @pl.when((p >= first_pair) & (p < first_pair + n_pairs))
        def _():
            @pl.when(first_chip & ((core == 0) | (k == 0)))
            def _():
                prepare(k, p)

            @pl.when(k != core)
            def _():
                swap_wait(1, k, p)

            work(k, p)

        return carry

    lax.fori_loop(0, 2 * (even + core * (PAIRS - even - few)), step, 0)

    for i in range(5):
        part_copy(i, core).wait_send()

    @pl.when(has_right)
    def _():
        for i in range(3):
            head_copy(core, i).wait_send()

    def sent(ref, send, there):
        @pl.when(there)
        def _():
            remote(ref, ref, send, out_recv, other).wait_send()

    for n in sorted({few, even, PAIRS - few}):
        sent(flow.at[0, pl.ds(0, n)], swap_send.at[0], far_pairs == n)
        sent(flow.at[pl.ds(0, 2), pl.ds(0, 2 * n)], swap_send.at[1], far_pairs == n)
        these = n_pairs == n
        sent(state_out.at[:, pl.ds(0, 2 * n)], state_send, these & has_right)
        sent(edge_out.at[1, pl.ds(0, 2 * n)], edge_send.at[1], these & has_right)
        sent(edge_out.at[0, pl.ds(0, 2 * n)], edge_send.at[0], these & has_right & has_down)
        sent(flow.at[0, pl.ds(0, 2 * n)], prev_send, these & has_down)
        sent(flow.at[0, pl.ds(0, 2 * n)], out_send, these)

        @pl.when(far_pairs == n)
        def _(n=n):
            ref = flow.at[0, pl.ds(0, 2 * n)]
            remote(ref, ref, out_send, out_recv, other).wait_recv()


def solution(mesh):
    stages, ranges = mesh.shape["pipe"] // 2, mesh.shape["ctx"]
    f32, bf16 = jnp.float32, jnp.bfloat16
    vmem = pl.BlockSpec(memory_space=pltpu.VMEM)
    hbm = pl.BlockSpec(memory_space=pltpu.HBM)
    dma = pltpu.SemaphoreType.DMA
    pin = functools.partial(pltpu.with_memory_space_constraint, memory_space=pltpu.HBM)

    def on_device(x, gate, bc, dt, rate, weight, skip, gain):
        channels = x.shape[3] + bc.shape[3]
        return pl.pallas_call(
            functools.partial(kernel, stages, ranges),
            out_shape=jax.ShapeDtypeStruct(x.shape, bf16),
            in_specs=[hbm] * 8,
            out_specs=vmem,
            scratch_shapes=[
                pltpu.VMEM((1, SEQS, HEADS, BLOCK), f32),
                pltpu.VMEM(rate.shape, f32),
                pltpu.VMEM(skip.shape, f32),
                pltpu.VMEM((2,) + weight.shape[1:], f32),
                pltpu.VMEM((2,) + gain.shape, f32),
                pltpu.VMEM((2,) + x.shape[1:], bf16),
                pltpu.VMEM((2,) + gate.shape[1:], bf16),
                pltpu.VMEM((2,) + bc.shape[1:], bf16),
                pltpu.VMEM((2, UNITS // 4, BLOCK, BLOCK), bf16),
                pltpu.VMEM((2, BLOCK, PER_GROUP * HALF), bf16),
                pltpu.VMEM((2, ROWS, BLOCK), bf16),
                pltpu.VMEM((BLOCK, BLOCK), f32),
                pltpu.VMEM((3 * 32, PER_GROUP * HALF), bf16),
                pltpu.VMEM((HALF, PER_GROUP * HALF), bf16),
                pltpu.VMEM((2 * BLOCK, 2 * WIDTH), bf16),
                pltpu.VMEM((2, UNITS, BLOCK, PER_GROUP * HALF), bf16),
                pltpu.VMEM((2, UNITS, 2, STATE, HALF), bf16),
                pltpu.VMEM((2, UNITS, BLOCK, STATE), bf16),
                pltpu.VMEM((2, UNITS, BLOCK + EDGE, WIDTH), f32),
                pltpu.VMEM((2, UNITS, BLOCK, WIDTH), bf16),
                pltpu.VMEM((4, PAD + BLOCK, BLOCK), f32),
                pltpu.VMEM((2, PAD + BLOCK, 2 * STATE), f32),
                pltpu.VMEM((SEQS, EDGE, FOLD), bf16),
                pltpu.VMEM((2, SEQS, EDGE, FOLD), bf16),
                pltpu.VMEM((2, SEQS * PAD, channels), f32),
                pltpu.VMEM((3, UNITS, BLOCK, WIDTH), bf16),
                pltpu.VMEM((2, UNITS, PAD, BLOCK), f32),
                pltpu.VMEM((2, UNITS, PAD, BLOCK), f32),
                pltpu.VMEM((2, UNITS, STATE, WIDTH), bf16),
                pltpu.VMEM((2, UNITS, STATE, WIDTH), bf16),
                dma((8,)),
                dma((5,)),
                dma((5,)),
                dma((2,)),
                dma((2, PAIRS)),
                dma((3,)),
                dma((2, SEQS)),
                dma(()),
                dma((PAIRS,)),
                dma((2,)),
                dma((2, PAIRS)),
                dma(()),
                dma((2, UNITS)),
                dma(()),
                dma(()),
            ],
            compiler_params=pltpu.CompilerParams(
                collective_id=0, has_side_effects=True, vmem_limit_bytes=52 * 1024 * 1024
            ),
            name="relay",
        )(*map(pin, (x, gate, bc, jnp.swapaxes(dt, 2, 3), rate, weight, skip, gain)))

    rows = P("pipe", None, "ctx", None)
    in_specs = (rows, rows, rows, rows, P("pipe", None), P("pipe", None, None), P("pipe", None), P("pipe", None))
    return jax.shard_map(on_device, mesh=mesh, in_specs=in_specs, out_specs=rows, check_vma=False)
```

```python
import functools

import jax
import jax.numpy as jnp
from jax import lax
from jax.experimental import pallas as pl
from jax.experimental.pallas import tpu as pltpu
from jax.sharding import PartitionSpec as P

HEADS = 64
HEAD_DIM = 32
GROUPS = 8
STATE = 64
BLOCK = 128
HALF = BLOCK // 2
SEQS = 2
PER_GROUP = HEADS // GROUPS
WIDTH = PER_GROUP * HEAD_DIM
HD = HEADS * HEAD_DIM
UNITS = SEQS * GROUPS
PAIRS = UNITS // 2
EDGE = 16
PAD = 8
KEPT = 4
FOLD = (HD + 2 * GROUPS * STATE) * KEPT // EDGE
TAPS = 4
GANG = 1
FEW = 6
EVEN = 8
ROWS = 2 * BLOCK + EDGE

norm_eps = 1e-05
MESH = pl.DeviceIdType.MESH
HIGHEST = lax.Precision.HIGHEST
LOG2E = 1.4426950408889634


def silu_of_twice(half):
    return half * jnp.tanh(half) + half


def conv(buf, weight):
    first = PAD - TAPS + 1
    halves = 0.5 * weight
    total = halves[0:1] * buf[first : first + BLOCK]
    for tap in range(1, TAPS):
        total = total + halves[tap : tap + 1] * buf[first + tap : first + tap + BLOCK]
    return silu_of_twice(total)


def pieces(v):
    parts = []
    for _ in range(3):
        part = v.astype(jnp.bfloat16).astype(jnp.float32)
        parts.append(part)
        v = v - part
    return parts


def kernel(
    stages,
    ranges,
    x_hbm,
    gate_hbm,
    bc_hbm,
    dt_hbm,
    rate_hbm,
    w_hbm,
    skip_hbm,
    gain_hbm,
    out_ref,
    dt_ref,
    rate_ref,
    skip_ref,
    w_buf,
    gain_buf,
    x_buf,
    gate_buf,
    bc_buf,
    lead_buf,
    key_buf,
    pair_buf,
    keys,
    chosen,
    masked,
    shifted,
    weights,
    b_rows,
    c_rows,
    wides,
    tails,
    opened,
    cbuf,
    bbuf,
    head_out,
    head_in,
    heads,
    flow,
    edge,
    edge_out,
    state_in,
    state_out,
    fetch_sem,
    part_send,
    part_recv,
    swap_send,
    swap_recv,
    head_send,
    head_recv,
    prev_send,
    prev_recv,
    edge_send,
    edge_recv,
    state_send,
    state_recv,
    out_send,
    out_recv,
):
    f32, bf16 = jnp.float32, jnp.bfloat16
    section = lax.axis_index("pipe")
    mine = lax.axis_index("ctx")
    stage, core = section // 2, section % 2
    other = 2 * stage + 1 - core
    has_down = stage < stages - 1
    has_up = stage > 0
    has_right = mine < ranges - 1
    has_left = mine > 0
    first_chip = (stage == 0) & (mine == 0)

    def share(at_stage, at_range):
        return jnp.maximum(FEW, EVEN - (EVEN - FEW) * (at_range // 2 + at_stage))

    def owner(u, at_stage, at_range):
        return 2 * at_stage + (u >= share(at_stage, at_range)).astype(jnp.int32)

    shared = share(stage, mine)
    low = core * shared
    many = shared + core * (UNITS - 2 * shared)
    first_pair, n_pairs = low // 2, many // 2
    far_pair, far_pairs = (1 - core) * (shared // 2), PAIRS - n_pairs

    fetches = [
        pltpu.make_async_copy(src, dst, fetch_sem.at[i])
        for i, (src, dst) in enumerate(
            (
                (dt_hbm, dt_ref),
                (rate_hbm, rate_ref),
                (skip_hbm, skip_ref),
                (bc_hbm.at[0], bc_buf.at[core]),
                (x_hbm.at[0], x_buf.at[core]),
                (w_hbm.at[0], w_buf.at[core]),
                (gain_hbm, gain_buf.at[core]),
                (gate_hbm.at[0], gate_buf.at[core]),
            )
        )
    ]
    for fetch in fetches:
        fetch.start()

    barrier = pltpu.get_barrier_semaphore()
    partners = [(core >= 0, other, 0)]
    for there, down, along in (
        (has_right, 0, 1),
        (has_left, 0, -1),
        (has_down, 1, 0),
        (has_up, -1, 0),
        (has_down & has_right, 1, 1),
        (has_up & has_left, -1, -1),
    ):
        for side in range(2):
            partners.append((there, 2 * (stage + down) + side, along))
    count = 0
    for there, to, along in partners:
        count = count + there.astype(jnp.int32)

        @pl.when(there)
        def _(to=to, along=along):
            pl.semaphore_signal(
                barrier,
                inc=1,
                device_id={"pipe": to, "ctx": mine + along},
                device_id_type=MESH,
            )

    def remote(src, dst, send, recv, to, along=0):
        return pltpu.make_async_remote_copy(
            src_ref=src,
            dst_ref=dst,
            send_sem=send,
            recv_sem=recv,
            device_id={"pipe": to, "ctx": mine + along},
            device_id_type=MESH,
        )

    def part_copy(i, k):
        src, dst = (
            (lead_buf.at[k], lead_buf),
            (key_buf.at[k], key_buf),
            (pair_buf.at[k], pair_buf),
            (w_hbm.at[0], w_buf),
            (gain_hbm, gain_buf),
        )[i]
        return remote(src, dst.at[k], part_send.at[i], part_recv.at[i], other)

    def swap_copy(kind, k, p):
        s, at = p // (GROUPS // 2), p % (GROUPS // 2)
        if kind < 2:
            lanes = pl.ds(pl.multiple_of(kind * GROUPS * STATE + at * 2 * STATE, 2 * STATE), 2 * STATE)
            src, dst = bc_hbm, bc_buf
        else:
            lanes = pl.ds(pl.multiple_of(at * 2 * WIDTH, 2 * WIDTH), 2 * WIDTH)
            src, dst = ((x_hbm, x_buf), (gate_hbm, gate_buf))[kind - 2]
        return remote(
            src.at[0, s, :, lanes],
            dst.at[k, s, :, lanes],
            swap_send.at[kind // 2],
            swap_recv.at[kind // 2, p],
            other,
        )

    def swap_wait(half, k, p):
        ref = (bc_buf.at[k, 0, :, pl.ds(0, 4 * STATE)], x_buf.at[k, 0, :, pl.ds(0, 4 * WIDTH)])[half]
        remote(ref, ref, swap_send.at[half], swap_recv.at[half, p], other).wait_recv()

    HEAD_PARTS = ((0, 0), (0, 1), (1, 1))

    def head_copy(k, i):
        s, side = HEAD_PARTS[i]
        return remote(
            head_out.at[s],
            head_in.at[k, s],
            head_send.at[i],
            head_recv.at[k, s],
            2 * stage + side,
            1,
        )

    def prev_copy(u):
        gang = pl.ds(u, GANG)
        return remote(
            flow.at[2, gang], flow.at[0, gang], prev_send, prev_recv.at[u], owner(u, stage + 1, mine)
        )

    def edge_copy(k, u):
        gang = pl.ds(u, GANG)
        return remote(
            edge_out.at[k, gang],
            edge.at[k, gang],
            edge_send.at[k],
            edge_recv.at[k, u],
            owner(u, stage + 1 - k, mine + 1),
            1,
        )

    def state_copy(k, u):
        return remote(
            state_out.at[k, u],
            state_in.at[k, u],
            state_send,
            state_recv.at[k, u],
            owner(u, stage, mine + 1),
            1,
        )

    def out_copy(k, u):
        lanes = pl.ds(pl.multiple_of((u % GROUPS) * WIDTH, WIDTH), WIDTH)
        return remote(
            flow.at[k + 1, u],
            out_ref.at[0, u // GROUPS, :, lanes],
            out_send,
            out_recv,
            other,
        )

    sh_rows = lax.broadcasted_iota(jnp.int32, (2 * BLOCK, 2 * WIDTH), 0)
    sh_cols = lax.broadcasted_iota(jnp.int32, (2 * BLOCK, 2 * WIDTH), 1)
    shifted[...] = (sh_rows == BLOCK + sh_cols // HEAD_DIM).astype(bf16)
    ch_rows = lax.broadcasted_iota(jnp.int32, (3 * 32, PER_GROUP * HALF), 0)
    ch_cols = lax.broadcasted_iota(jnp.int32, (3 * 32, PER_GROUP * HALF), 1)
    chosen[...] = (ch_rows % PER_GROUP == ch_cols // HALF).astype(bf16)
    masked[...] = jnp.where(ch_rows[:HALF] < ch_cols[:HALF] % HALF, -1e30, 0.0).astype(bf16)

    for fetch in fetches[:3]:
        fetch.wait()
    rows = lax.broadcasted_iota(jnp.int32, (BLOCK, BLOCK), 0)
    cols = lax.broadcasted_iota(jnp.int32, (BLOCK, BLOCK), 1)
    raw = jnp.concatenate([dt_ref[0, s] for s in range(SEQS)], axis=0)
    steps = jnp.maximum(raw, 0.0) + jnp.log1p(jnp.exp(-jnp.abs(raw)))
    rates = jnp.concatenate([rate_ref[...]] * SEQS, axis=1)
    rates = jnp.broadcast_to(rates, (BLOCK, SEQS * HEADS)).T
    summed = jnp.dot(
        -steps * rates,
        (rows <= cols).astype(f32),
        precision=HIGHEST,
        preferred_element_type=f32,
    )
    keys[...] = summed * LOG2E - jnp.log2(steps)
    left = cols < HALF
    one_keys, two_keys = [], []
    for q in range(PER_GROUP // 2):
        one = keys[pl.ds(2 * q, UNITS, stride=PER_GROUP), :]
        two = keys[pl.ds(2 * q + 1, UNITS, stride=PER_GROUP), :]
        one_keys.append(jnp.where(left[:UNITS], one, pltpu.roll(two, HALF, 1)))
        two_keys.append(jnp.where(left[:UNITS], pltpu.roll(one, HALF, 1), two))
    stacked = jnp.concatenate(
        pieces(jnp.concatenate(one_keys, axis=1)) + pieces(jnp.concatenate(two_keys, axis=1)), axis=0
    ).astype(bf16)
    order = ((cols // UNITS == rows % PER_GROUP) & (cols % UNITS == rows // PER_GROUP))[:, : 6 * UNITS]
    key_buf[core] = jnp.dot(
        order.astype(bf16), stacked, preferred_element_type=f32
    ).astype(bf16)
    cum = summed.T
    slot = cols % PER_GROUP
    halves = jnp.where((slot < 6) & (slot // 3 == rows // HALF), -1.0, 0.0)
    leads = pieces(cum * LOG2E)
    for quad in range(UNITS // 4):
        lead = halves
        for i in (2, 1, 0):
            turn = (32 * (i - quad)) % BLOCK
            part = pltpu.roll(leads[i], turn, 1) if turn else leads[i]
            lead = jnp.where(cols < 32 * (i + 1), part, lead)
        lead_buf[core, quad] = lead.astype(bf16)
    middle, end = cum[HALF - 1 : HALF], cum[BLOCK - 1 : BLOCK]
    grown = jnp.exp(jnp.where(rows < HALF, cum, cum - middle))
    tail = jnp.exp(jnp.where(rows < HALF, middle, end) - cum) * steps.T
    skips = jnp.concatenate([skip_ref[...]] * SEQS, axis=1)
    extra = jnp.zeros((EDGE, BLOCK), f32)
    slot = rows[:EDGE]
    for i, row in enumerate((skips, grown[HALF - 1 : HALF], grown[BLOCK - 1 : BLOCK])):
        row_high = row.astype(bf16).astype(f32)
        extra = jnp.where(slot == 2 * i, row_high, extra)
        extra = jnp.where(slot == 2 * i + 1, row - row_high, extra)
    pair_buf[core] = jnp.concatenate([grown, extra, tail], axis=0).astype(bf16)

    fetches[3].wait()
    fetches[4].wait()
    for s in range(SEQS):
        last = jnp.concatenate(
            [
                ref[core, s, BLOCK - EDGE :, :].astype(f32)[EDGE - KEPT :]
                for ref in (x_buf, bc_buf)
            ],
            axis=1,
        )
        head_out[s] = jnp.concatenate(
            [last[:, m * FOLD : (m + 1) * FOLD] for m in range(EDGE // KEPT)], axis=0
        ).astype(bf16)
    pl.semaphore_wait(barrier, count)

    @pl.when(has_right)
    def _():
        for i in range(3):
            head_copy(core, i).start()

    for i in range(4):
        part_copy(i, core).start()

    def swap(p, carry):
        for kind in range(4):
            swap_copy(kind, core, p).start()
        return carry

    lax.fori_loop(far_pair, far_pair + far_pairs, swap, 0)
    part_copy(4, core).start()

    @pl.when(jnp.logical_not(has_left))
    def _():
        heads[...] = jnp.zeros_like(heads)

    @pl.when(has_left)
    def _():
        def unfold(k, s):
            folded = head_in[k, s].astype(f32)
            for m in range(EDGE // KEPT):
                heads[k, s * PAD + PAD - KEPT : (s + 1) * PAD, m * FOLD : (m + 1) * FOLD] = folded[
                    m * KEPT : (m + 1) * KEPT
                ]

        for k in range(2):
            head_copy(k, 0).wait_recv()
            unfold(k, 0)

            @pl.when(core == 1)
            def _(k=k):
                head_copy(k, 2).wait_recv()
                unfold(k, 1)

    fetches[5].wait()
    left = left[:HALF]
    unit_of = cols % 32 // PER_GROUP
    token_of = (rows % HALF == cols)[:, :HALF].astype(bf16)

    def prepare(k, p):
        @pl.when(k != core)
        def _():
            @pl.when(p == first_pair)
            def _():
                for i in range(5):
                    part_copy(i, k).wait_recv()

            swap_wait(0, k, p)

        s, pair = p // (GROUPS // 2), p % (GROUPS // 2)
        acts = []
        for part in range(2):
            at = pl.multiple_of(part * GROUPS * STATE + pair * 2 * STATE, 2 * STATE)
            wide = pl.ds(pl.multiple_of(HD + at, 2 * STATE), 2 * STATE)
            bbuf[part, pl.ds(0, PAD), :] = heads[k, pl.ds(pl.multiple_of(s * PAD, PAD), PAD), wide]
            bbuf[part, pl.ds(PAD, BLOCK), :] = bc_buf[k, s, :, pl.ds(at, 2 * STATE)].astype(f32)
            acts.append(conv(bbuf.at[part], w_buf[k, :, wide]).astype(bf16))
        b_t = acts[0].astype(f32).T
        quad = p // 2
        lead = lead_buf[k, quad]
        chooser = jnp.concatenate(
            [chosen[...], key_buf[k, pl.ds(pl.multiple_of(quad * 32, 32), 32), :], masked[...]], axis=0
        )
        lead_rows = [
            jnp.where(unit_of == (2 * p + half) % 4, lead, jnp.zeros_like(lead)) for half in range(2)
        ]
        gap = jnp.dot(
            jnp.concatenate(
                [jnp.concatenate(lead_rows, axis=0), jnp.concatenate([token_of] * 2, axis=0)], axis=1
            ),
            chooser,
            preferred_element_type=f32,
        )
        spread = shifted[pl.ds(pl.multiple_of(BLOCK - 2 * PER_GROUP * p, 2 * PER_GROUP), BLOCK), :]
        wide = jnp.dot(pair_buf[k], spread, preferred_element_type=f32)
        for half in range(2):
            u = 2 * p + half
            c_u = acts[1][:, half * STATE : (half + 1) * STATE]
            b_u = b_t[half * STATE : (half + 1) * STATE]
            b_turned = pltpu.roll(b_u, HALF, 1)
            b_one = jnp.where(left, b_u, b_turned).astype(bf16)
            b_two = jnp.where(left, b_turned, b_u).astype(bf16)
            c_rows[k, u] = c_u
            b_rows[k, u, 0] = b_one[:, :HALF]
            b_rows[k, u, 1] = b_two[:, :HALF]
            scores = (
                jnp.dot(c_u[:HALF], b_one, preferred_element_type=f32),
                jnp.dot(c_u[HALF:], b_two, preferred_element_type=f32),
            )
            for part in range(2):
                tokens = slice(part * HALF, (part + 1) * HALF)
                gap_rows = slice((2 * half + part) * HALF, (2 * half + part + 1) * HALF)
                for q in range(PER_GROUP // 2):
                    lanes = slice(q * BLOCK, (q + 1) * BLOCK)
                    weights[k, u, tokens, lanes] = (
                        scores[part] * jnp.exp2(gap[gap_rows, lanes])
                    ).astype(bf16)
            here = slice(half * WIDTH, (half + 1) * WIDTH)
            wides[k, u] = wide[: BLOCK + EDGE, here]
            tails[k, u] = wide[BLOCK + EDGE :, here].astype(bf16)

    def ahead(i, carry):
        turn = i // n_pairs
        k = core + turn * (1 - 2 * core)
        prepare(k, first_pair + i % n_pairs)
        return carry

    lazy = first_chip.astype(jnp.int32)
    lax.fori_loop(0, n_pairs * (2 - lazy) - lazy * (1 - core) * (n_pairs - 2), ahead, 0)

    fetches[6].wait()
    fetches[7].wait()
    lane_head = lax.broadcasted_iota(jnp.int32, (HALF, BLOCK), 1) // HEAD_DIM

    def work(k, first):
        s = first // GROUPS
        gang = tuple(first + i for i in range(GANG))

        def lanes_of(u, side=0, width=WIDTH):
            return pl.ds(pl.multiple_of((u % GROUPS) * WIDTH + side * width, width), width)

        @pl.when((k == 0) & has_up)
        def _():
            prev_copy(first).wait_recv()

        @pl.when(has_left & ((k == 1) | has_up))
        def _():
            edge_copy(k, first).wait_recv()

        @pl.when((k == 0) & jnp.logical_not(has_up))
        def _():
            for u in gang:
                flow[0, u] = jnp.zeros(flow.shape[2:], bf16)

        @pl.when(jnp.logical_not(has_left & ((k == 1) | has_up)))
        def _():
            for u in gang:
                edge[k, u] = jnp.zeros(edge.shape[2:], f32)

        @pl.when(jnp.logical_not(has_left))
        def _():
            for u in gang:
                state_in[k, u] = jnp.zeros(state_in.shape[2:], bf16)

        xs_of, falls, locals_one, locals_all, mixed_of = [], [], [], [], []
        for i, u in enumerate(gang):
            gate = (0.5 * gate_buf[k, s, :, lanes_of(u)]).astype(f32)
            opened[i] = silu_of_twice(gate)
        for i, u in enumerate(gang):
            sides = []
            for side in range(2):
                at = lanes_of(u, side, BLOCK)
                buf = cbuf.at[2 * i + side]
                buf[pl.ds(0, PAD), :] = heads[k, pl.ds(pl.multiple_of(s * PAD, PAD), PAD), at]
                buf[pl.ds(PAD - KEPT, KEPT), :] += edge[k, u, side * KEPT : (side + 1) * KEPT]
                buf[pl.ds(PAD, BLOCK), :] = x_buf[k, s, :, at].astype(f32) + flow[
                    k, u, :, side * BLOCK : (side + 1) * BLOCK
                ].astype(f32)
                sides.append(conv(buf, w_buf[k, :, at]).astype(bf16))
            xs = jnp.concatenate(sides, axis=1)
            xs_of.append(xs)
            keyed = xs * tails[k, u]
            extra = wides[k, u, BLOCK : BLOCK + PAD]
            fall_one, fall_two = extra[2:3] + extra[3:4], extra[4:5] + extra[5:6]
            local_one = jnp.dot(b_rows[k, u, 0], keyed[:HALF], preferred_element_type=f32)
            local_two = jnp.dot(b_rows[k, u, 1], keyed[HALF:], preferred_element_type=f32)
            falls.append((fall_one, fall_two))
            locals_one.append(local_one)
            locals_all.append(fall_two * local_one + local_two)
        zero = jnp.zeros((HALF, BLOCK), bf16)
        for u, xs in zip(gang, xs_of):
            mixed = []
            for part in range(2):
                tokens = slice(part * HALF, (part + 1) * HALF)
                sides = []
                for side in range(2):
                    xs_side = xs[tokens, side * BLOCK : (side + 1) * BLOCK]
                    diagonal = jnp.concatenate(
                        [jnp.where(lane_head == h, xs_side, zero) for h in range(PER_GROUP // 2)],
                        axis=0,
                    )
                    sides.append(
                        jnp.dot(
                            weights[k, u, tokens, side * WIDTH : (side + 1) * WIDTH],
                            diagonal,
                            preferred_element_type=f32,
                        )
                    )
                mixed.append(jnp.concatenate(sides, axis=1))
            skip = wides[k, u, BLOCK : BLOCK + 1] + wides[k, u, BLOCK + 1 : BLOCK + 2]
            mixed_of.append(jnp.concatenate(mixed, axis=0) + skip * xs.astype(f32))

        arrived = []
        for i, u in enumerate(gang):

            @pl.when(has_left)
            def _(u=u):
                state_copy(k, u).wait_recv()

            incoming = state_in[k, u].astype(f32)
            fall_one, fall_two = falls[i]
            state_out[k, u] = ((fall_one * fall_two) * incoming + locals_all[i]).astype(bf16)
            arrived.append(incoming)

            @pl.when(has_right)
            def _(u=u):
                state_copy(k, u).start()

        for i, u in enumerate(gang):
            incoming = arrived[i]
            between = (falls[i][0] * incoming + locals_one[i]).astype(bf16)
            off = jnp.concatenate(
                [
                    jnp.dot(c_rows[k, u, :HALF], incoming.astype(bf16), preferred_element_type=f32),
                    jnp.dot(c_rows[k, u, HALF:], between, preferred_element_type=f32),
                ],
                axis=0,
            )
            mixed = mixed_of[i] + off * wides[k, u, :BLOCK]
            gated = mixed * opened[i]
            mean = jnp.sum(gated * gated, axis=1, keepdims=True) * (1.0 / WIDTH)
            result = (
                gated * lax.rsqrt(mean + norm_eps) * gain_buf[k, 0:1, lanes_of(u)]
            ).astype(bf16)
            flow[k + 1, u] = result
            last = result[BLOCK - EDGE :].astype(f32)[EDGE - KEPT :]
            edge_out[1 - k, u] = jnp.concatenate([last[:, :BLOCK], last[:, BLOCK:]], axis=0)

        @pl.when(has_right & ((k == 0) | has_down))
        def _():
            edge_copy(1 - k, first).start()

        @pl.when((k == 1) & has_down)
        def _():
            prev_copy(first).start()

        @pl.when(k == core)
        def _():
            for u in gang:
                out_ref[0, s, :, lanes_of(u)] = flow[k + 1, u]

        @pl.when(k != core)
        def _():
            for u in gang:
                out_copy(k, u).start()

    few, even, all_gangs = FEW // GANG, EVEN // GANG, UNITS // GANG

    def step(i, carry):
        k, i = i % 2, i // 2
        later = jnp.maximum(i - few, 0)
        u = GANG * jnp.where(
            core == 0,
            i,
            jnp.where(i < few, even + i, few + later // 2 + even * (1 - later % 2)),
        )
        p = u // 2

        @pl.when((u >= low) & (u < low + many))
        def _():
            @pl.when(first_chip & ((k != core) | ((core == 0) & (p >= 2))) & (u % 2 == 0))
            def _():
                prepare(k, p)

            @pl.when((k != core) & (u % 2 == 0))
            def _():
                swap_wait(1, k, p)

            work(k, u)

        return carry

    lax.fori_loop(0, 2 * (even + core * (all_gangs - even - few)), step, 0)

    for i in range(5):
        part_copy(i, core).wait_send()

    @pl.when(has_right)
    def _():
        for i in range(3):
            head_copy(core, i).wait_send()

    def sent(ref, send, there):
        @pl.when(there)
        def _():
            remote(ref, ref, send, out_recv, other).wait_send()

    for n in sorted({FEW // 2, EVEN // 2, PAIRS - FEW // 2}):
        sent(flow.at[0, pl.ds(0, n)], swap_send.at[0], far_pairs == n)
        sent(flow.at[pl.ds(0, 2), pl.ds(0, 2 * n)], swap_send.at[1], far_pairs == n)
        these = n_pairs == n
        sent(state_out.at[:, pl.ds(0, 2 * n)], state_send, these & has_right)
        sent(edge_out.at[1, pl.ds(0, 2 * n)], edge_send.at[1], these & has_right)
        sent(edge_out.at[0, pl.ds(0, 2 * n)], edge_send.at[0], these & has_right & has_down)
        sent(flow.at[0, pl.ds(0, 2 * n)], prev_send, these & has_down)
        sent(flow.at[0, pl.ds(0, 2 * n)], out_send, these)

        @pl.when(far_pairs == n)
        def _(n=n):
            ref = flow.at[0, pl.ds(0, 2 * n)]
            remote(ref, ref, out_send, out_recv, other).wait_recv()


def solution(mesh):
    stages, ranges = mesh.shape["pipe"] // 2, mesh.shape["ctx"]
    f32, bf16 = jnp.float32, jnp.bfloat16
    vmem = pl.BlockSpec(memory_space=pltpu.VMEM)
    hbm = pl.BlockSpec(memory_space=pltpu.HBM)
    dma = pltpu.SemaphoreType.DMA
    pin = functools.partial(pltpu.with_memory_space_constraint, memory_space=pltpu.HBM)

    def on_device(x, gate, bc, dt, rate, weight, skip, gain):
        channels = x.shape[3] + bc.shape[3]
        return pl.pallas_call(
            functools.partial(kernel, stages, ranges),
            out_shape=jax.ShapeDtypeStruct(x.shape, bf16),
            in_specs=[hbm] * 8,
            out_specs=vmem,
            scratch_shapes=[
                pltpu.VMEM((1, SEQS, HEADS, BLOCK), f32),
                pltpu.VMEM(rate.shape, f32),
                pltpu.VMEM(skip.shape, f32),
                pltpu.VMEM((2,) + weight.shape[1:], f32),
                pltpu.VMEM((2,) + gain.shape, f32),
                pltpu.VMEM((2,) + x.shape[1:], bf16),
                pltpu.VMEM((2,) + gate.shape[1:], bf16),
                pltpu.VMEM((2,) + bc.shape[1:], bf16),
                pltpu.VMEM((2, UNITS // 4, BLOCK, BLOCK), bf16),
                pltpu.VMEM((2, BLOCK, PER_GROUP * HALF), bf16),
                pltpu.VMEM((2, ROWS, BLOCK), bf16),
                pltpu.VMEM((BLOCK, BLOCK), f32),
                pltpu.VMEM((3 * 32, PER_GROUP * HALF), bf16),
                pltpu.VMEM((HALF, PER_GROUP * HALF), bf16),
                pltpu.VMEM((2 * BLOCK, 2 * WIDTH), bf16),
                pltpu.VMEM((2, UNITS, BLOCK, PER_GROUP * HALF), bf16),
                pltpu.VMEM((2, UNITS, 2, STATE, HALF), bf16),
                pltpu.VMEM((2, UNITS, BLOCK, STATE), bf16),
                pltpu.VMEM((2, UNITS, BLOCK + EDGE, WIDTH), f32),
                pltpu.VMEM((2, UNITS, BLOCK, WIDTH), bf16),
                pltpu.VMEM((GANG, BLOCK, WIDTH), f32),
                pltpu.VMEM((2 * GANG, PAD + BLOCK, BLOCK), f32),
                pltpu.VMEM((2, PAD + BLOCK, 2 * STATE), f32),
                pltpu.VMEM((SEQS, EDGE, FOLD), bf16),
                pltpu.VMEM((2, SEQS, EDGE, FOLD), bf16),
                pltpu.VMEM((2, SEQS * PAD, channels), f32),
                pltpu.VMEM((3, UNITS, BLOCK, WIDTH), bf16),
                pltpu.VMEM((2, UNITS, PAD, BLOCK), f32),
                pltpu.VMEM((2, UNITS, PAD, BLOCK), f32),
                pltpu.VMEM((2, UNITS, STATE, WIDTH), bf16),
                pltpu.VMEM((2, UNITS, STATE, WIDTH), bf16),
                dma((8,)),
                dma((5,)),
                dma((5,)),
                dma((2,)),
                dma((2, PAIRS)),
                dma((3,)),
                dma((2, SEQS)),
                dma(()),
                dma((UNITS,)),
                dma((2,)),
                dma((2, UNITS)),
                dma(()),
                dma((2, UNITS)),
                dma(()),
                dma(()),
            ],
            compiler_params=pltpu.CompilerParams(
                collective_id=0, has_side_effects=True, vmem_limit_bytes=52 * 1024 * 1024
            ),
            name="relay",
        )(*map(pin, (x, gate, bc, jnp.swapaxes(dt, 2, 3), rate, weight, skip, gain)))

    rows = P("pipe", None, "ctx", None)
    in_specs = (rows, rows, rows, rows, P("pipe", None), P("pipe", None, None), P("pipe", None), P("pipe", None))
    return jax.shard_map(on_device, mesh=mesh, in_specs=in_specs, out_specs=rows, check_vma=False)
```

```python
import functools

import jax
import jax.numpy as jnp
from jax import lax
from jax.experimental import pallas as pl
from jax.experimental.pallas import tpu as pltpu
from jax.sharding import PartitionSpec as P

HEADS = 64
HEAD_DIM = 32
GROUPS = 8
STATE = 64
BLOCK = 128
HALF = BLOCK // 2
SEQS = 2
PER_GROUP = HEADS // GROUPS
WIDTH = PER_GROUP * HEAD_DIM
HD = HEADS * HEAD_DIM
UNITS = SEQS * GROUPS
PAIRS = UNITS // 2
EDGE = 16
PAD = 8
KEPT = 4
FOLD = (HD + 2 * GROUPS * STATE) * KEPT // EDGE
TAPS = 4
GANG = 1
FEW = 6
EVEN = 8
MOST = max(EVEN, UNITS - FEW)
ROWS = 2 * BLOCK + EDGE

norm_eps = 1e-05
MESH = pl.DeviceIdType.MESH
HIGHEST = lax.Precision.HIGHEST
LOG2E = 1.4426950408889634


def silu_of_twice(half):
    return half * jnp.tanh(half) + half


def conv(buf, weight):
    first = PAD - TAPS + 1
    halves = 0.5 * weight
    total = halves[0:1] * buf[first : first + BLOCK]
    for tap in range(1, TAPS):
        total = total + halves[tap : tap + 1] * buf[first + tap : first + tap + BLOCK]
    return silu_of_twice(total)


def pieces(v):
    parts = []
    for _ in range(3):
        part = v.astype(jnp.bfloat16).astype(jnp.float32)
        parts.append(part)
        v = v - part
    return parts


def kernel(
    stages,
    ranges,
    x_hbm,
    gate_hbm,
    bc_hbm,
    dt_hbm,
    rate_hbm,
    w_hbm,
    skip_hbm,
    gain_hbm,
    out_ref,
    dt_ref,
    rate_ref,
    skip_ref,
    w_buf,
    gain_buf,
    x_buf,
    gate_buf,
    bc_buf,
    lead_buf,
    key_buf,
    pair_buf,
    keys,
    chosen,
    masked,
    shifted,
    weights,
    b_rows,
    c_rows,
    wides,
    tails,
    opened,
    cbuf,
    bbuf,
    head_out,
    head_in,
    heads,
    flow,
    edge,
    edge_out,
    state_in,
    state_out,
    fetch_sem,
    part_send,
    part_recv,
    swap_send,
    swap_recv,
    head_send,
    head_recv,
    prev_send,
    prev_recv,
    edge_send,
    edge_recv,
    state_send,
    state_recv,
    out_send,
    out_recv,
):
    f32, bf16 = jnp.float32, jnp.bfloat16
    section = lax.axis_index("pipe")
    mine = lax.axis_index("ctx")
    stage, core = section // 2, section % 2
    other = 2 * stage + 1 - core
    has_down = stage < stages - 1
    has_up = stage > 0
    has_right = mine < ranges - 1
    has_left = mine > 0
    first_chip = (stage == 0) & (mine == 0)

    def share(at_stage, at_range):
        return jnp.maximum(FEW, EVEN - (EVEN - FEW) * (at_range // 2 + at_stage))

    def owner(u, at_stage, at_range):
        return 2 * at_stage + (u >= share(at_stage, at_range)).astype(jnp.int32)

    def place(u, at_stage, at_range):
        most = share(at_stage, at_range)
        return u - most * (u >= most).astype(jnp.int32)

    shared = share(stage, mine)
    low = core * shared
    many = shared + core * (UNITS - 2 * shared)
    first_pair, n_pairs = low // 2, many // 2
    far_pair, far_pairs = (1 - core) * (shared // 2), PAIRS - n_pairs

    fetches = [
        pltpu.make_async_copy(src, dst, fetch_sem.at[i])
        for i, (src, dst) in enumerate(
            (
                (dt_hbm, dt_ref),
                (rate_hbm, rate_ref),
                (skip_hbm, skip_ref),
                (bc_hbm.at[0], bc_buf.at[core]),
                (x_hbm.at[0], x_buf.at[core]),
                (w_hbm.at[0], w_buf.at[core]),
                (gain_hbm, gain_buf.at[core]),
                (gate_hbm.at[0], gate_buf.at[core]),
            )
        )
    ]
    for fetch in fetches:
        fetch.start()

    barrier = pltpu.get_barrier_semaphore()
    partners = [(core >= 0, other, 0)]
    for there, down, along in (
        (has_right, 0, 1),
        (has_left, 0, -1),
        (has_down, 1, 0),
        (has_up, -1, 0),
        (has_down & has_right, 1, 1),
        (has_up & has_left, -1, -1),
    ):
        for side in range(2):
            partners.append((there, 2 * (stage + down) + side, along))
    count = 0
    for there, to, along in partners:
        count = count + there.astype(jnp.int32)

        @pl.when(there)
        def _(to=to, along=along):
            pl.semaphore_signal(
                barrier,
                inc=1,
                device_id={"pipe": to, "ctx": mine + along},
                device_id_type=MESH,
            )

    def remote(src, dst, send, recv, to, along=0):
        return pltpu.make_async_remote_copy(
            src_ref=src,
            dst_ref=dst,
            send_sem=send,
            recv_sem=recv,
            device_id={"pipe": to, "ctx": mine + along},
            device_id_type=MESH,
        )

    def part_copy(i, k):
        src, dst = (
            (lead_buf.at[k], lead_buf),
            (key_buf.at[k], key_buf),
            (pair_buf.at[k], pair_buf),
            (w_hbm.at[0], w_buf),
            (gain_hbm, gain_buf),
        )[i]
        return remote(src, dst.at[k], part_send.at[i], part_recv.at[i], other)

    def swap_copy(kind, k, p, first):
        s, at = p // (GROUPS // 2), p % (GROUPS // 2)
        if kind < 2:
            lanes = pl.ds(pl.multiple_of(kind * GROUPS * STATE + at * 2 * STATE, 2 * STATE), 2 * STATE)
            src, dst = bc_hbm, bc_buf
        else:
            lanes = pl.ds(pl.multiple_of(at * 2 * WIDTH, 2 * WIDTH), 2 * WIDTH)
            src, dst = ((x_hbm, x_buf), (gate_hbm, gate_buf))[kind - 2]
        return remote(
            src.at[0, s, :, lanes],
            dst.at[k, s, :, lanes],
            swap_send.at[kind // 2],
            swap_recv.at[kind // 2, p - first],
            other,
        )

    def swap_wait(half, k, p):
        ref = (bc_buf.at[k, 0, :, pl.ds(0, 4 * STATE)], x_buf.at[k, 0, :, pl.ds(0, 4 * WIDTH)])[half]
        remote(ref, ref, swap_send.at[half], swap_recv.at[half, p - first_pair], other).wait_recv()

    HEAD_PARTS = ((0, 0), (0, 1), (1, 1))

    def head_copy(k, i):
        s, side = HEAD_PARTS[i]
        return remote(
            head_out.at[s],
            head_in.at[k, s],
            head_send.at[i],
            head_recv.at[k, s],
            2 * stage + side,
            1,
        )

    def prev_copy(u, side, down=1):
        lanes = pl.ds(side * BLOCK, BLOCK)
        return remote(
            flow.at[2, u, :, lanes],
            flow.at[0, u, :, lanes],
            prev_send,
            prev_recv.at[place(u, stage + down, mine), side],
            owner(u, stage + 1, mine),
        )

    def edge_copy(k, u, down=0, along=0):
        return remote(
            edge_out.at[k, u],
            edge.at[k, u],
            edge_send.at[k],
            edge_recv.at[k, place(u, stage + down, mine + along)],
            owner(u, stage + 1 - k, mine + 1),
            1,
        )

    def state_copy(k, u, side, along=1):
        return remote(
            state_out.at[k, u, side],
            state_in.at[k, u, side],
            state_send,
            state_recv.at[k, place(u, stage, mine + along), side],
            owner(u, stage, mine + 1),
            1,
        )

    def out_copy(k, u):
        lanes = pl.ds(pl.multiple_of((u % GROUPS) * WIDTH, WIDTH), WIDTH)
        return remote(
            flow.at[k + 1, u],
            out_ref.at[0, u // GROUPS, :, lanes],
            out_send,
            out_recv,
            other,
        )

    sh_rows = lax.broadcasted_iota(jnp.int32, (2 * BLOCK, 2 * WIDTH), 0)
    sh_cols = lax.broadcasted_iota(jnp.int32, (2 * BLOCK, 2 * WIDTH), 1)
    shifted[...] = (sh_rows == BLOCK + sh_cols // HEAD_DIM).astype(bf16)
    ch_rows = lax.broadcasted_iota(jnp.int32, (3 * 32, PER_GROUP * HALF), 0)
    ch_cols = lax.broadcasted_iota(jnp.int32, (3 * 32, PER_GROUP * HALF), 1)
    chosen[...] = (ch_rows % PER_GROUP == ch_cols // HALF).astype(bf16)
    masked[...] = jnp.where(ch_rows[:HALF] < ch_cols[:HALF] % HALF, -1e30, 0.0).astype(bf16)

    for fetch in fetches[:3]:
        fetch.wait()
    rows = lax.broadcasted_iota(jnp.int32, (BLOCK, BLOCK), 0)
    cols = lax.broadcasted_iota(jnp.int32, (BLOCK, BLOCK), 1)
    raw = jnp.concatenate([dt_ref[0, s] for s in range(SEQS)], axis=0)
    steps = jnp.maximum(raw, 0.0) + jnp.log1p(jnp.exp(-jnp.abs(raw)))
    rates = jnp.concatenate([rate_ref[...]] * SEQS, axis=1)
    rates = jnp.broadcast_to(rates, (BLOCK, SEQS * HEADS)).T
    summed = jnp.dot(
        -steps * rates,
        (rows <= cols).astype(f32),
        precision=HIGHEST,
        preferred_element_type=f32,
    )
    keys[...] = summed * LOG2E - jnp.log2(steps)
    left = cols < HALF
    one_keys, two_keys = [], []
    for q in range(PER_GROUP // 2):
        one = keys[pl.ds(2 * q, UNITS, stride=PER_GROUP), :]
        two = keys[pl.ds(2 * q + 1, UNITS, stride=PER_GROUP), :]
        one_keys.append(jnp.where(left[:UNITS], one, pltpu.roll(two, HALF, 1)))
        two_keys.append(jnp.where(left[:UNITS], pltpu.roll(one, HALF, 1), two))
    stacked = jnp.concatenate(
        pieces(jnp.concatenate(one_keys, axis=1)) + pieces(jnp.concatenate(two_keys, axis=1)), axis=0
    ).astype(bf16)
    order = ((cols // UNITS == rows % PER_GROUP) & (cols % UNITS == rows // PER_GROUP))[:, : 6 * UNITS]
    key_buf[core] = jnp.dot(
        order.astype(bf16), stacked, preferred_element_type=f32
    ).astype(bf16)
    cum = summed.T
    slot = cols % PER_GROUP
    halves = jnp.where((slot < 6) & (slot // 3 == rows // HALF), -1.0, 0.0)
    leads = pieces(cum * LOG2E)
    for quad in range(UNITS // 4):
        lead = halves
        for i in (2, 1, 0):
            turn = (32 * (i - quad)) % BLOCK
            part = pltpu.roll(leads[i], turn, 1) if turn else leads[i]
            lead = jnp.where(cols < 32 * (i + 1), part, lead)
        lead_buf[core, quad] = lead.astype(bf16)
    middle, end = cum[HALF - 1 : HALF], cum[BLOCK - 1 : BLOCK]
    grown = jnp.exp(jnp.where(rows < HALF, cum, cum - middle))
    tail = jnp.exp(jnp.where(rows < HALF, middle, end) - cum) * steps.T
    skips = jnp.concatenate([skip_ref[...]] * SEQS, axis=1)
    extra = jnp.zeros((EDGE, BLOCK), f32)
    slot = rows[:EDGE]
    for i, row in enumerate((skips, grown[HALF - 1 : HALF], grown[BLOCK - 1 : BLOCK])):
        row_high = row.astype(bf16).astype(f32)
        extra = jnp.where(slot == 2 * i, row_high, extra)
        extra = jnp.where(slot == 2 * i + 1, row - row_high, extra)
    pair_buf[core] = jnp.concatenate([grown, extra, tail], axis=0).astype(bf16)

    fetches[3].wait()
    fetches[4].wait()
    for s in range(SEQS):
        last = jnp.concatenate(
            [
                ref[core, s, BLOCK - EDGE :, :].astype(f32)[EDGE - KEPT :]
                for ref in (x_buf, bc_buf)
            ],
            axis=1,
        )
        head_out[s] = jnp.concatenate(
            [last[:, m * FOLD : (m + 1) * FOLD] for m in range(EDGE // KEPT)], axis=0
        ).astype(bf16)
    pl.semaphore_wait(barrier, count)

    @pl.when(has_right)
    def _():
        for i in range(3):
            head_copy(core, i).start()

    for i in range(4):
        part_copy(i, core).start()

    def swap(p, carry):
        for kind in range(4):
            swap_copy(kind, core, p, far_pair).start()
        return carry

    lax.fori_loop(far_pair, far_pair + far_pairs, swap, 0)
    part_copy(4, core).start()

    @pl.when(jnp.logical_not(has_left))
    def _():
        heads[...] = jnp.zeros_like(heads)

    @pl.when(has_left)
    def _():
        def unfold(k, s):
            folded = head_in[k, s].astype(f32)
            for m in range(EDGE // KEPT):
                heads[k, s * PAD + PAD - KEPT : (s + 1) * PAD, m * FOLD : (m + 1) * FOLD] = folded[
                    m * KEPT : (m + 1) * KEPT
                ]

        for k in range(2):
            head_copy(k, 0).wait_recv()
            unfold(k, 0)

            @pl.when(core == 1)
            def _(k=k):
                head_copy(k, 2).wait_recv()
                unfold(k, 1)

    fetches[5].wait()
    left = left[:HALF]
    unit_of = cols % 32 // PER_GROUP
    token_of = (rows % HALF == cols)[:, :HALF].astype(bf16)

    def prepare(k, p):
        @pl.when(k != core)
        def _():
            @pl.when(p == first_pair)
            def _():
                for i in range(5):
                    part_copy(i, k).wait_recv()

            swap_wait(0, k, p)

        s, pair = p // (GROUPS // 2), p % (GROUPS // 2)
        acts = []
        for part in range(2):
            at = pl.multiple_of(part * GROUPS * STATE + pair * 2 * STATE, 2 * STATE)
            wide = pl.ds(pl.multiple_of(HD + at, 2 * STATE), 2 * STATE)
            bbuf[part, pl.ds(0, PAD), :] = heads[k, pl.ds(pl.multiple_of(s * PAD, PAD), PAD), wide]
            bbuf[part, pl.ds(PAD, BLOCK), :] = bc_buf[k, s, :, pl.ds(at, 2 * STATE)].astype(f32)
            acts.append(conv(bbuf.at[part], w_buf[k, :, wide]).astype(bf16))
        b_t = acts[0].astype(f32).T
        quad = p // 2
        lead = lead_buf[k, quad]
        chooser = jnp.concatenate(
            [chosen[...], key_buf[k, pl.ds(pl.multiple_of(quad * 32, 32), 32), :], masked[...]], axis=0
        )
        lead_rows = [
            jnp.where(unit_of == (2 * p + half) % 4, lead, jnp.zeros_like(lead)) for half in range(2)
        ]
        gap = jnp.dot(
            jnp.concatenate(
                [jnp.concatenate(lead_rows, axis=0), jnp.concatenate([token_of] * 2, axis=0)], axis=1
            ),
            chooser,
            preferred_element_type=f32,
        )
        spread = shifted[pl.ds(pl.multiple_of(BLOCK - 2 * PER_GROUP * p, 2 * PER_GROUP), BLOCK), :]
        wide = jnp.dot(pair_buf[k], spread, preferred_element_type=f32)
        for half in range(2):
            u = 2 * p + half
            c_u = acts[1][:, half * STATE : (half + 1) * STATE]
            b_u = b_t[half * STATE : (half + 1) * STATE]
            b_turned = pltpu.roll(b_u, HALF, 1)
            b_one = jnp.where(left, b_u, b_turned).astype(bf16)
            b_two = jnp.where(left, b_turned, b_u).astype(bf16)
            c_rows[k, u] = c_u
            b_rows[k, u, 0] = b_one[:, :HALF]
            b_rows[k, u, 1] = b_two[:, :HALF]
            scores = (
                jnp.dot(c_u[:HALF], b_one, preferred_element_type=f32),
                jnp.dot(c_u[HALF:], b_two, preferred_element_type=f32),
            )
            for part in range(2):
                tokens = slice(part * HALF, (part + 1) * HALF)
                gap_rows = slice((2 * half + part) * HALF, (2 * half + part + 1) * HALF)
                for q in range(PER_GROUP // 2):
                    lanes = slice(q * BLOCK, (q + 1) * BLOCK)
                    weights[k, u, tokens, lanes] = (
                        scores[part] * jnp.exp2(gap[gap_rows, lanes])
                    ).astype(bf16)
            here = slice(half * WIDTH, (half + 1) * WIDTH)
            wides[k, u] = wide[: BLOCK + EDGE, here]
            tails[k, u] = wide[BLOCK + EDGE :, here].astype(bf16)

    def ahead(i, carry):
        turn = i // n_pairs
        k = core + turn * (1 - 2 * core)
        prepare(k, first_pair + i % n_pairs)
        return carry

    lazy = first_chip.astype(jnp.int32)
    lax.fori_loop(0, n_pairs * (2 - lazy) - lazy * (1 - core) * (n_pairs - 2), ahead, 0)

    fetches[6].wait()
    fetches[7].wait()
    lane_head = lax.broadcasted_iota(jnp.int32, (HALF, BLOCK), 1) // HEAD_DIM

    def work(k, first):
        s = first // GROUPS
        gang = tuple(first + i for i in range(GANG))

        def lanes_of(u, side=0, width=WIDTH):
            return pl.ds(pl.multiple_of((u % GROUPS) * WIDTH + side * width, width), width)

        @pl.when(has_left & ((k == 1) | has_up))
        def _():
            for u in gang:
                edge_copy(k, u).wait_recv()

        @pl.when((k == 0) & jnp.logical_not(has_up))
        def _():
            for u in gang:
                flow[0, u] = jnp.zeros(flow.shape[2:], bf16)

        @pl.when(jnp.logical_not(has_left & ((k == 1) | has_up)))
        def _():
            for u in gang:
                edge[k, u] = jnp.zeros(edge.shape[2:], f32)

        @pl.when(jnp.logical_not(has_left))
        def _():
            for u in gang:
                state_in[k, u] = jnp.zeros(state_in.shape[2:], bf16)

        xs_of, falls, locals_one, locals_all, mixed_of = [], [], [], [], []
        for i, u in enumerate(gang):
            gate = (0.5 * gate_buf[k, s, :, lanes_of(u)]).astype(f32)
            opened[i] = silu_of_twice(gate)
        for i, u in enumerate(gang):
            sides = []
            for side in range(2):

                @pl.when((k == 0) & has_up)
                def _(u=u, side=side):
                    prev_copy(u, side, 0).wait_recv()

                at = lanes_of(u, side, BLOCK)
                buf = cbuf.at[2 * i + side]
                buf[pl.ds(0, PAD), :] = heads[k, pl.ds(pl.multiple_of(s * PAD, PAD), PAD), at]
                buf[pl.ds(PAD - KEPT, KEPT), :] += edge[k, u, side * KEPT : (side + 1) * KEPT]
                buf[pl.ds(PAD, BLOCK), :] = x_buf[k, s, :, at].astype(f32) + flow[
                    k, u, :, side * BLOCK : (side + 1) * BLOCK
                ].astype(f32)
                sides.append(conv(buf, w_buf[k, :, at]).astype(bf16))
            xs = jnp.concatenate(sides, axis=1)
            xs_of.append(xs)
            keyed = xs * tails[k, u]
            extra = wides[k, u, BLOCK : BLOCK + PAD]
            fall_one, fall_two = extra[2:3] + extra[3:4], extra[4:5] + extra[5:6]
            local_one = jnp.dot(b_rows[k, u, 0], keyed[:HALF], preferred_element_type=f32)
            local_two = jnp.dot(b_rows[k, u, 1], keyed[HALF:], preferred_element_type=f32)
            falls.append((fall_one, fall_two))
            locals_one.append(local_one)
            locals_all.append(fall_two * local_one + local_two)
        zero = jnp.zeros((HALF, BLOCK), bf16)
        for u, xs in zip(gang, xs_of):
            mixed = []
            for part in range(2):
                tokens = slice(part * HALF, (part + 1) * HALF)
                sides = []
                for side in range(2):
                    xs_side = xs[tokens, side * BLOCK : (side + 1) * BLOCK]
                    diagonal = jnp.concatenate(
                        [jnp.where(lane_head == h, xs_side, zero) for h in range(PER_GROUP // 2)],
                        axis=0,
                    )
                    sides.append(
                        jnp.dot(
                            weights[k, u, tokens, side * WIDTH : (side + 1) * WIDTH],
                            diagonal,
                            preferred_element_type=f32,
                        )
                    )
                mixed.append(jnp.concatenate(sides, axis=1))
            skip = wides[k, u, BLOCK : BLOCK + 1] + wides[k, u, BLOCK + 1 : BLOCK + 2]
            mixed_of.append(jnp.concatenate(mixed, axis=0) + skip * xs.astype(f32))

        arrived = []
        for i, u in enumerate(gang):
            fall_one, fall_two = falls[i]
            fall = fall_one * fall_two
            sides = []
            for side in range(2):

                @pl.when(has_left)
                def _(u=u, side=side):
                    state_copy(k, u, side, 0).wait_recv()

                here = slice(side * BLOCK, (side + 1) * BLOCK)
                incoming = state_in[k, u, side].astype(f32)
                state_out[k, u, side] = (fall[:, here] * incoming + locals_all[i][:, here]).astype(
                    bf16
                )
                sides.append(incoming)

                @pl.when(has_right)
                def _(u=u, side=side):
                    state_copy(k, u, side).start()

            arrived.append(jnp.concatenate(sides, axis=1))

        for i, u in enumerate(gang):
            incoming = arrived[i]
            between = (falls[i][0] * incoming + locals_one[i]).astype(bf16)
            off = jnp.concatenate(
                [
                    jnp.dot(c_rows[k, u, :HALF], incoming.astype(bf16), preferred_element_type=f32),
                    jnp.dot(c_rows[k, u, HALF:], between, preferred_element_type=f32),
                ],
                axis=0,
            )
            mixed = mixed_of[i] + off * wides[k, u, :BLOCK]
            gated = mixed * opened[i]
            mean = jnp.sum(gated * gated, axis=1, keepdims=True) * (1.0 / WIDTH)
            result = (
                gated * lax.rsqrt(mean + norm_eps) * gain_buf[k, 0:1, lanes_of(u)]
            ).astype(bf16)
            flow[k + 1, u] = result
            last = result[BLOCK - EDGE :].astype(f32)[EDGE - KEPT :]
            edge_out[1 - k, u] = jnp.concatenate([last[:, :BLOCK], last[:, BLOCK:]], axis=0)

        @pl.when(has_right & ((k == 0) | has_down))
        def _():
            for u in gang:
                edge_copy(1 - k, u, k, 1).start()

        @pl.when((k == 1) & has_down)
        def _():
            for u in gang:
                for side in range(2):
                    prev_copy(u, side).start()

        @pl.when(k == core)
        def _():
            for u in gang:
                out_ref[0, s, :, lanes_of(u)] = flow[k + 1, u]

        @pl.when(k != core)
        def _():
            for u in gang:
                out_copy(k, u).start()

    few, even, all_gangs = FEW // GANG, EVEN // GANG, UNITS // GANG

    def step(i, carry):
        k, i = i % 2, i // 2
        later = jnp.maximum(i - few, 0)
        u = GANG * jnp.where(
            core == 0,
            i,
            jnp.where(i < few, even + i, few + later // 2 + even * (1 - later % 2)),
        )
        p = u // 2

        @pl.when((u >= low) & (u < low + many))
        def _():
            @pl.when(first_chip & ((k != core) | ((core == 0) & (p >= 2))) & (u % 2 == 0))
            def _():
                prepare(k, p)

            @pl.when((k != core) & (u % 2 == 0))
            def _():
                swap_wait(1, k, p)

            work(k, u)

        return carry

    lax.fori_loop(0, 2 * (even + core * (all_gangs - even - few)), step, 0)

    for i in range(5):
        part_copy(i, core).wait_send()

    @pl.when(has_right)
    def _():
        for i in range(3):
            head_copy(core, i).wait_send()

    def sent(ref, send, there):
        @pl.when(there)
        def _():
            remote(ref, ref, send, out_recv, other).wait_send()

    for n in sorted({FEW // 2, EVEN // 2, PAIRS - FEW // 2}):
        sent(flow.at[0, pl.ds(0, n)], swap_send.at[0], far_pairs == n)
        sent(flow.at[pl.ds(0, 2), pl.ds(0, 2 * n)], swap_send.at[1], far_pairs == n)
        these = n_pairs == n
        sent(state_out.at[:, pl.ds(0, 2 * n)], state_send, these & has_right)
        sent(edge_out.at[1, pl.ds(0, 2 * n)], edge_send.at[1], these & has_right)
        sent(edge_out.at[0, pl.ds(0, 2 * n)], edge_send.at[0], these & has_right & has_down)
        sent(flow.at[0, pl.ds(0, 2 * n)], prev_send, these & has_down)
        sent(flow.at[0, pl.ds(0, 2 * n)], out_send, these)

        @pl.when(far_pairs == n)
        def _(n=n):
            ref = flow.at[0, pl.ds(0, 2 * n)]
            remote(ref, ref, out_send, out_recv, other).wait_recv()


def solution(mesh):
    stages, ranges = mesh.shape["pipe"] // 2, mesh.shape["ctx"]
    f32, bf16 = jnp.float32, jnp.bfloat16
    vmem = pl.BlockSpec(memory_space=pltpu.VMEM)
    hbm = pl.BlockSpec(memory_space=pltpu.HBM)
    dma = pltpu.SemaphoreType.DMA
    pin = functools.partial(pltpu.with_memory_space_constraint, memory_space=pltpu.HBM)

    def on_device(x, gate, bc, dt, rate, weight, skip, gain):
        channels = x.shape[3] + bc.shape[3]
        return pl.pallas_call(
            functools.partial(kernel, stages, ranges),
            out_shape=jax.ShapeDtypeStruct(x.shape, bf16),
            in_specs=[hbm] * 8,
            out_specs=vmem,
            scratch_shapes=[
                pltpu.VMEM((1, SEQS, HEADS, BLOCK), f32),
                pltpu.VMEM(rate.shape, f32),
                pltpu.VMEM(skip.shape, f32),
                pltpu.VMEM((2,) + weight.shape[1:], f32),
                pltpu.VMEM((2,) + gain.shape, f32),
                pltpu.VMEM((2,) + x.shape[1:], bf16),
                pltpu.VMEM((2,) + gate.shape[1:], bf16),
                pltpu.VMEM((2,) + bc.shape[1:], bf16),
                pltpu.VMEM((2, UNITS // 4, BLOCK, BLOCK), bf16),
                pltpu.VMEM((2, BLOCK, PER_GROUP * HALF), bf16),
                pltpu.VMEM((2, ROWS, BLOCK), bf16),
                pltpu.VMEM((BLOCK, BLOCK), f32),
                pltpu.VMEM((3 * 32, PER_GROUP * HALF), bf16),
                pltpu.VMEM((HALF, PER_GROUP * HALF), bf16),
                pltpu.VMEM((2 * BLOCK, 2 * WIDTH), bf16),
                pltpu.VMEM((2, UNITS, BLOCK, PER_GROUP * HALF), bf16),
                pltpu.VMEM((2, UNITS, 2, STATE, HALF), bf16),
                pltpu.VMEM((2, UNITS, BLOCK, STATE), bf16),
                pltpu.VMEM((2, UNITS, BLOCK + EDGE, WIDTH), f32),
                pltpu.VMEM((2, UNITS, BLOCK, WIDTH), bf16),
                pltpu.VMEM((GANG, BLOCK, WIDTH), f32),
                pltpu.VMEM((2 * GANG, PAD + BLOCK, BLOCK), f32),
                pltpu.VMEM((2, PAD + BLOCK, 2 * STATE), f32),
                pltpu.VMEM((SEQS, EDGE, FOLD), bf16),
                pltpu.VMEM((2, SEQS, EDGE, FOLD), bf16),
                pltpu.VMEM((2, SEQS * PAD, channels), f32),
                pltpu.VMEM((3, UNITS, BLOCK, WIDTH), bf16),
                pltpu.VMEM((2, UNITS, PAD, BLOCK), f32),
                pltpu.VMEM((2, UNITS, PAD, BLOCK), f32),
                pltpu.VMEM((2, UNITS, 2, STATE, BLOCK), bf16),
                pltpu.VMEM((2, UNITS, 2, STATE, BLOCK), bf16),
                dma((8,)),
                dma((5,)),
                dma((5,)),
                dma((2,)),
                dma((2, MOST // 2)),
                dma((3,)),
                dma((2, SEQS)),
                dma(()),
                dma((MOST, 2)),
                dma((2,)),
                dma((2, MOST)),
                dma(()),
                dma((2, MOST, 2)),
                dma(()),
                dma(()),
            ],
            compiler_params=pltpu.CompilerParams(
                collective_id=0, has_side_effects=True, vmem_limit_bytes=52 * 1024 * 1024
            ),
            name="relay",
        )(*map(pin, (x, gate, bc, jnp.swapaxes(dt, 2, 3), rate, weight, skip, gain)))

    rows = P("pipe", None, "ctx", None)
    in_specs = (rows, rows, rows, rows, P("pipe", None), P("pipe", None, None), P("pipe", None), P("pipe", None))
    return jax.shard_map(on_device, mesh=mesh, in_specs=in_specs, out_specs=rows, check_vma=False)
```

```python
import functools

import jax
import jax.numpy as jnp
from jax import lax
from jax.experimental import pallas as pl
from jax.experimental.pallas import tpu as pltpu
from jax.sharding import PartitionSpec as P

HEADS = 64
HEAD_DIM = 32
GROUPS = 8
STATE = 64
BLOCK = 128
HALF = BLOCK // 2
SEQS = 2
PER_GROUP = HEADS // GROUPS
WIDTH = PER_GROUP * HEAD_DIM
HD = HEADS * HEAD_DIM
UNITS = SEQS * GROUPS
PAIRS = UNITS // 2
EDGE = 16
PAD = 8
KEPT = 4
FOLD = (HD + 2 * GROUPS * STATE) * KEPT // EDGE
TAPS = 4
GANG = 1
FEW = 6
EVEN = 8
MOST = max(EVEN, UNITS - FEW)
ROWS = 2 * BLOCK + EDGE

norm_eps = 1e-05
MESH = pl.DeviceIdType.MESH
HIGHEST = lax.Precision.HIGHEST
LOG2E = 1.4426950408889634


def silu_of_twice(half):
    return half * jnp.tanh(half) + half


def conv(buf, weight):
    first = PAD - TAPS + 1
    halves = 0.5 * weight
    total = halves[0:1] * buf[first : first + BLOCK]
    for tap in range(1, TAPS):
        total = total + halves[tap : tap + 1] * buf[first + tap : first + tap + BLOCK]
    return silu_of_twice(total)


def pieces(v):
    parts = []
    for _ in range(3):
        part = v.astype(jnp.bfloat16).astype(jnp.float32)
        parts.append(part)
        v = v - part
    return parts


def kernel(
    stages,
    ranges,
    x_hbm,
    gate_hbm,
    bc_hbm,
    dt_hbm,
    rate_hbm,
    w_hbm,
    skip_hbm,
    gain_hbm,
    out_ref,
    dt_ref,
    rate_ref,
    skip_ref,
    w_buf,
    gain_buf,
    x_buf,
    gate_buf,
    bc_buf,
    lead_buf,
    key_buf,
    pair_buf,
    keys,
    chosen,
    masked,
    shifted,
    weights,
    b_rows,
    c_rows,
    wides,
    tails,
    opened,
    cbuf,
    bbuf,
    head_out,
    head_in,
    heads,
    flow,
    edge,
    edge_out,
    state_in,
    state_out,
    fetch_sem,
    part_send,
    part_recv,
    swap_send,
    swap_recv,
    head_send,
    head_recv,
    prev_send,
    prev_recv,
    edge_send,
    edge_recv,
    state_send,
    state_recv,
    out_send,
    out_recv,
):
    f32, bf16 = jnp.float32, jnp.bfloat16
    section = lax.axis_index("pipe")
    mine = lax.axis_index("ctx")
    stage, core = section // 2, section % 2
    other = 2 * stage + 1 - core
    has_down = stage < stages - 1
    has_up = stage > 0
    has_right = mine < ranges - 1
    has_left = mine > 0
    first_chip = (stage == 0) & (mine == 0)

    def share(at_stage, at_range):
        return jnp.maximum(FEW, EVEN - (EVEN - FEW) * (at_range // 2 + at_stage))

    def owner(u, at_stage, at_range):
        return 2 * at_stage + (u >= share(at_stage, at_range)).astype(jnp.int32)

    def place(u, at_stage, at_range):
        most = share(at_stage, at_range)
        return u - most * (u >= most).astype(jnp.int32)

    shared = share(stage, mine)
    low = core * shared
    many = shared + core * (UNITS - 2 * shared)
    first_pair, n_pairs = low // 2, many // 2
    far_pair, far_pairs = (1 - core) * (shared // 2), PAIRS - n_pairs

    fetches = [
        pltpu.make_async_copy(src, dst, fetch_sem.at[i])
        for i, (src, dst) in enumerate(
            (
                (dt_hbm, dt_ref),
                (rate_hbm, rate_ref),
                (skip_hbm, skip_ref),
                (bc_hbm.at[0], bc_buf.at[core]),
                (x_hbm.at[0], x_buf.at[core]),
                (w_hbm.at[0], w_buf.at[core]),
                (gain_hbm, gain_buf.at[core]),
                (gate_hbm.at[0], gate_buf.at[core]),
            )
        )
    ]
    for fetch in fetches:
        fetch.start()

    barrier = pltpu.get_barrier_semaphore()
    partners = [(core >= 0, other, 0)]
    for there, down, along in (
        (has_right, 0, 1),
        (has_left, 0, -1),
        (has_down, 1, 0),
        (has_up, -1, 0),
    ):
        for side in range(2):
            partners.append((there, 2 * (stage + down) + side, along))
    count = 0
    for there, to, along in partners:
        count = count + there.astype(jnp.int32)

        @pl.when(there)
        def _(to=to, along=along):
            pl.semaphore_signal(
                barrier,
                inc=1,
                device_id={"pipe": to, "ctx": mine + along},
                device_id_type=MESH,
            )

    def remote(src, dst, send, recv, to, along=0):
        return pltpu.make_async_remote_copy(
            src_ref=src,
            dst_ref=dst,
            send_sem=send,
            recv_sem=recv,
            device_id={"pipe": to, "ctx": mine + along},
            device_id_type=MESH,
        )

    def part_copy(i, k):
        src, dst = (
            (lead_buf.at[k], lead_buf),
            (key_buf.at[k], key_buf),
            (pair_buf.at[k], pair_buf),
            (w_hbm.at[0], w_buf),
            (gain_hbm, gain_buf),
        )[i]
        return remote(src, dst.at[k], part_send.at[i], part_recv.at[i], other)

    def swap_copy(kind, k, p, first):
        s, at = p // (GROUPS // 2), p % (GROUPS // 2)
        if kind < 2:
            lanes = pl.ds(pl.multiple_of(kind * GROUPS * STATE + at * 2 * STATE, 2 * STATE), 2 * STATE)
            src, dst = bc_hbm, bc_buf
        else:
            lanes = pl.ds(pl.multiple_of(at * 2 * WIDTH, 2 * WIDTH), 2 * WIDTH)
            src, dst = ((x_hbm, x_buf), (gate_hbm, gate_buf))[kind - 2]
        return remote(
            src.at[0, s, :, lanes],
            dst.at[k, s, :, lanes],
            swap_send.at[kind // 2],
            swap_recv.at[kind // 2, p - first],
            other,
        )

    def swap_wait(half, k, p):
        ref = (bc_buf.at[k, 0, :, pl.ds(0, 4 * STATE)], x_buf.at[k, 0, :, pl.ds(0, 4 * WIDTH)])[half]
        remote(ref, ref, swap_send.at[half], swap_recv.at[half, p - first_pair], other).wait_recv()

    HEAD_PARTS = ((0, 0), (0, 1), (1, 1))

    def head_copy(k, i):
        s, side = HEAD_PARTS[i]
        return remote(
            head_out.at[s],
            head_in.at[k, s],
            head_send.at[i],
            head_recv.at[k, s],
            2 * stage + side,
            1,
        )

    def prev_copy(u, down=1):
        return remote(
            flow.at[2, u],
            flow.at[0, u],
            prev_send,
            prev_recv.at[place(u, stage + down, mine)],
            owner(u, stage + 1, mine),
        )

    def edge_copy(k, u, along=0):
        return remote(
            edge_out.at[k, u],
            edge.at[k, u],
            edge_send.at[k],
            edge_recv.at[k, place(u, stage, mine + along)],
            owner(u, stage, mine + 1),
            1,
        )

    def state_copy(k, u, along=1):
        return remote(
            state_out.at[k, u],
            state_in.at[k, u],
            state_send,
            state_recv.at[k, place(u, stage, mine + along)],
            owner(u, stage, mine + 1),
            1,
        )

    def out_copy(k, u):
        lanes = pl.ds(pl.multiple_of((u % GROUPS) * WIDTH, WIDTH), WIDTH)
        return remote(
            flow.at[k + 1, u],
            out_ref.at[0, u // GROUPS, :, lanes],
            out_send,
            out_recv,
            other,
        )

    sh_rows = lax.broadcasted_iota(jnp.int32, (2 * BLOCK, 2 * WIDTH), 0)
    sh_cols = lax.broadcasted_iota(jnp.int32, (2 * BLOCK, 2 * WIDTH), 1)
    shifted[...] = (sh_rows == BLOCK + sh_cols // HEAD_DIM).astype(bf16)
    ch_rows = lax.broadcasted_iota(jnp.int32, (3 * 32, PER_GROUP * HALF), 0)
    ch_cols = lax.broadcasted_iota(jnp.int32, (3 * 32, PER_GROUP * HALF), 1)
    chosen[...] = (ch_rows % PER_GROUP == ch_cols // HALF).astype(bf16)
    masked[...] = jnp.where(ch_rows[:HALF] < ch_cols[:HALF] % HALF, -1e30, 0.0).astype(bf16)

    for fetch in fetches[:3]:
        fetch.wait()
    rows = lax.broadcasted_iota(jnp.int32, (BLOCK, BLOCK), 0)
    cols = lax.broadcasted_iota(jnp.int32, (BLOCK, BLOCK), 1)
    raw = jnp.concatenate([dt_ref[0, s] for s in range(SEQS)], axis=0)
    steps = jnp.maximum(raw, 0.0) + jnp.log1p(jnp.exp(-jnp.abs(raw)))
    rates = jnp.concatenate([rate_ref[...]] * SEQS, axis=1)
    rates = jnp.broadcast_to(rates, (BLOCK, SEQS * HEADS)).T
    summed = jnp.dot(
        -steps * rates,
        (rows <= cols).astype(f32),
        precision=HIGHEST,
        preferred_element_type=f32,
    )
    keys[...] = summed * LOG2E - jnp.log2(steps)
    left = cols < HALF
    one_keys, two_keys = [], []
    for q in range(PER_GROUP // 2):
        one = keys[pl.ds(2 * q, UNITS, stride=PER_GROUP), :]
        two = keys[pl.ds(2 * q + 1, UNITS, stride=PER_GROUP), :]
        one_keys.append(jnp.where(left[:UNITS], one, pltpu.roll(two, HALF, 1)))
        two_keys.append(jnp.where(left[:UNITS], pltpu.roll(one, HALF, 1), two))
    stacked = jnp.concatenate(
        pieces(jnp.concatenate(one_keys, axis=1)) + pieces(jnp.concatenate(two_keys, axis=1)), axis=0
    ).astype(bf16)
    order = ((cols // UNITS == rows % PER_GROUP) & (cols % UNITS == rows // PER_GROUP))[:, : 6 * UNITS]
    key_buf[core] = jnp.dot(
        order.astype(bf16), stacked, preferred_element_type=f32
    ).astype(bf16)
    cum = summed.T
    slot = cols % PER_GROUP
    halves = jnp.where((slot < 6) & (slot // 3 == rows // HALF), -1.0, 0.0)
    leads = pieces(cum * LOG2E)
    for quad in range(UNITS // 4):
        lead = halves
        for i in (2, 1, 0):
            turn = (32 * (i - quad)) % BLOCK
            part = pltpu.roll(leads[i], turn, 1) if turn else leads[i]
            lead = jnp.where(cols < 32 * (i + 1), part, lead)
        lead_buf[core, quad] = lead.astype(bf16)
    middle, end = cum[HALF - 1 : HALF], cum[BLOCK - 1 : BLOCK]
    grown = jnp.exp(jnp.where(rows < HALF, cum, cum - middle))
    tail = jnp.exp(jnp.where(rows < HALF, middle, end) - cum) * steps.T
    skips = jnp.concatenate([skip_ref[...]] * SEQS, axis=1)
    extra = jnp.zeros((EDGE, BLOCK), f32)
    slot = rows[:EDGE]
    for i, row in enumerate((skips, grown[HALF - 1 : HALF], grown[BLOCK - 1 : BLOCK])):
        row_high = row.astype(bf16).astype(f32)
        extra = jnp.where(slot == 2 * i, row_high, extra)
        extra = jnp.where(slot == 2 * i + 1, row - row_high, extra)
    pair_buf[core] = jnp.concatenate([grown, extra, tail], axis=0).astype(bf16)

    fetches[3].wait()
    fetches[4].wait()
    for s in range(SEQS):
        last = jnp.concatenate(
            [
                ref[core, s, BLOCK - EDGE :, :].astype(f32)[EDGE - KEPT :]
                for ref in (x_buf, bc_buf)
            ],
            axis=1,
        )
        head_out[s] = jnp.concatenate(
            [last[:, m * FOLD : (m + 1) * FOLD] for m in range(EDGE // KEPT)], axis=0
        ).astype(bf16)
    pl.semaphore_wait(barrier, count)

    @pl.when(has_right)
    def _():
        for i in range(3):
            head_copy(core, i).start()

    for i in range(4):
        part_copy(i, core).start()

    def swap(p, carry):
        for kind in range(4):
            swap_copy(kind, core, p, far_pair).start()
        return carry

    lax.fori_loop(far_pair, far_pair + far_pairs, swap, 0)
    part_copy(4, core).start()

    @pl.when(jnp.logical_not(has_left))
    def _():
        heads[...] = jnp.zeros_like(heads)

    @pl.when(has_left)
    def _():
        def unfold(k, s):
            folded = head_in[k, s].astype(f32)
            for m in range(EDGE // KEPT):
                heads[k, s * PAD + PAD - KEPT : (s + 1) * PAD, m * FOLD : (m + 1) * FOLD] = folded[
                    m * KEPT : (m + 1) * KEPT
                ]

        for k in range(2):
            head_copy(k, 0).wait_recv()
            unfold(k, 0)

            @pl.when(core == 1)
            def _(k=k):
                head_copy(k, 2).wait_recv()
                unfold(k, 1)

    fetches[5].wait()
    left = left[:HALF]
    unit_of = cols % 32 // PER_GROUP
    token_of = (rows % HALF == cols)[:, :HALF].astype(bf16)

    def prepare(k, p):
        @pl.when(k != core)
        def _():
            @pl.when(p == first_pair)
            def _():
                for i in range(5):
                    part_copy(i, k).wait_recv()

            swap_wait(0, k, p)

        s, pair = p // (GROUPS // 2), p % (GROUPS // 2)
        acts = []
        for part in range(2):
            at = pl.multiple_of(part * GROUPS * STATE + pair * 2 * STATE, 2 * STATE)
            wide = pl.ds(pl.multiple_of(HD + at, 2 * STATE), 2 * STATE)
            bbuf[part, pl.ds(0, PAD), :] = heads[k, pl.ds(pl.multiple_of(s * PAD, PAD), PAD), wide]
            bbuf[part, pl.ds(PAD, BLOCK), :] = bc_buf[k, s, :, pl.ds(at, 2 * STATE)].astype(f32)
            acts.append(conv(bbuf.at[part], w_buf[k, :, wide]).astype(bf16))
        b_t = acts[0].astype(f32).T
        quad = p // 2
        lead = lead_buf[k, quad]
        chooser = jnp.concatenate(
            [chosen[...], key_buf[k, pl.ds(pl.multiple_of(quad * 32, 32), 32), :], masked[...]], axis=0
        )
        lead_rows = [
            jnp.where(unit_of == (2 * p + half) % 4, lead, jnp.zeros_like(lead)) for half in range(2)
        ]
        gap = jnp.dot(
            jnp.concatenate(
                [jnp.concatenate(lead_rows, axis=0), jnp.concatenate([token_of] * 2, axis=0)], axis=1
            ),
            chooser,
            preferred_element_type=f32,
        )
        spread = shifted[pl.ds(pl.multiple_of(BLOCK - 2 * PER_GROUP * p, 2 * PER_GROUP), BLOCK), :]
        wide = jnp.dot(pair_buf[k], spread, preferred_element_type=f32)
        for half in range(2):
            u = 2 * p + half
            c_u = acts[1][:, half * STATE : (half + 1) * STATE]
            b_u = b_t[half * STATE : (half + 1) * STATE]
            b_turned = pltpu.roll(b_u, HALF, 1)
            b_one = jnp.where(left, b_u, b_turned).astype(bf16)
            b_two = jnp.where(left, b_turned, b_u).astype(bf16)
            c_rows[k, u] = c_u
            b_rows[k, u, 0] = b_one[:, :HALF]
            b_rows[k, u, 1] = b_two[:, :HALF]
            scores = (
                jnp.dot(c_u[:HALF], b_one, preferred_element_type=f32),
                jnp.dot(c_u[HALF:], b_two, preferred_element_type=f32),
            )
            for part in range(2):
                tokens = slice(part * HALF, (part + 1) * HALF)
                gap_rows = slice((2 * half + part) * HALF, (2 * half + part + 1) * HALF)
                for q in range(PER_GROUP // 2):
                    lanes = slice(q * BLOCK, (q + 1) * BLOCK)
                    weights[k, u, tokens, lanes] = (
                        scores[part] * jnp.exp2(gap[gap_rows, lanes])
                    ).astype(bf16)
            here = slice(half * WIDTH, (half + 1) * WIDTH)
            wides[k, u] = wide[: BLOCK + EDGE, here]
            tails[k, u] = wide[BLOCK + EDGE :, here].astype(bf16)

    def ahead(i, carry):
        turn = i // n_pairs
        k = core + turn * (1 - 2 * core)
        prepare(k, first_pair + i % n_pairs)
        return carry

    lazy = first_chip.astype(jnp.int32)
    lax.fori_loop(0, n_pairs * (2 - lazy) - lazy * (1 - core) * (n_pairs - 2), ahead, 0)

    fetches[6].wait()
    fetches[7].wait()
    lane_head = lax.broadcasted_iota(jnp.int32, (HALF, BLOCK), 1) // HEAD_DIM

    def folded(tail):
        last = tail.astype(f32)[EDGE - KEPT :]
        return jnp.concatenate([last[:, :BLOCK], last[:, BLOCK:]], axis=0)

    def work(k, first):
        s = first // GROUPS
        gang = tuple(first + i for i in range(GANG))

        def lanes_of(u, side=0, width=WIDTH):
            return pl.ds(pl.multiple_of((u % GROUPS) * WIDTH + side * width, width), width)

        @pl.when((k == 0) & jnp.logical_not(has_up))
        def _():
            for u in gang:
                flow[0, u] = jnp.zeros(flow.shape[2:], bf16)

        @pl.when(jnp.logical_not(has_left & ((k == 1) | has_up)))
        def _():
            for u in gang:
                edge[k, u] = jnp.zeros(edge.shape[2:], f32)

        @pl.when(jnp.logical_not(has_left))
        def _():
            for u in gang:
                state_in[k, u] = jnp.zeros(state_in.shape[2:], bf16)

        xs_of, falls, locals_one, locals_all, mixed_of = [], [], [], [], []
        for i, u in enumerate(gang):
            gate = (0.5 * gate_buf[k, s, :, lanes_of(u)]).astype(f32)
            opened[i] = silu_of_twice(gate)
        for i, u in enumerate(gang):
            sides = []
            @pl.when((k == 0) & has_up)
            def _(u=u):
                prev_copy(u, 0).wait_recv()

            @pl.when((k == 0) & has_up & has_right)
            def _(u=u):
                edge_out[0, u] = folded(flow[0, u, BLOCK - EDGE :])
                edge_copy(0, u, 1).start()

            @pl.when(has_left & ((k == 1) | has_up))
            def _(u=u):
                edge_copy(k, u).wait_recv()

            for side in range(2):
                at = lanes_of(u, side, BLOCK)
                buf = cbuf.at[2 * i + side]
                buf[pl.ds(0, PAD), :] = heads[k, pl.ds(pl.multiple_of(s * PAD, PAD), PAD), at]
                buf[pl.ds(PAD - KEPT, KEPT), :] += edge[k, u, side * KEPT : (side + 1) * KEPT]
                buf[pl.ds(PAD, BLOCK), :] = x_buf[k, s, :, at].astype(f32) + flow[
                    k, u, :, side * BLOCK : (side + 1) * BLOCK
                ].astype(f32)
                sides.append(conv(buf, w_buf[k, :, at]).astype(bf16))
            xs = jnp.concatenate(sides, axis=1)
            xs_of.append(xs)
            keyed = xs * tails[k, u]
            extra = wides[k, u, BLOCK : BLOCK + PAD]
            fall_one, fall_two = extra[2:3] + extra[3:4], extra[4:5] + extra[5:6]
            local_one = jnp.dot(b_rows[k, u, 0], keyed[:HALF], preferred_element_type=f32)
            local_two = jnp.dot(b_rows[k, u, 1], keyed[HALF:], preferred_element_type=f32)
            falls.append((fall_one, fall_two))
            locals_one.append(local_one)
            locals_all.append(fall_two * local_one + local_two)
        zero = jnp.zeros((HALF, BLOCK), bf16)
        for u, xs in zip(gang, xs_of):
            mixed = []
            for part in range(2):
                tokens = slice(part * HALF, (part + 1) * HALF)
                sides = []
                for side in range(2):
                    xs_side = xs[tokens, side * BLOCK : (side + 1) * BLOCK]
                    diagonal = jnp.concatenate(
                        [jnp.where(lane_head == h, xs_side, zero) for h in range(PER_GROUP // 2)],
                        axis=0,
                    )
                    sides.append(
                        jnp.dot(
                            weights[k, u, tokens, side * WIDTH : (side + 1) * WIDTH],
                            diagonal,
                            preferred_element_type=f32,
                        )
                    )
                mixed.append(jnp.concatenate(sides, axis=1))
            skip = wides[k, u, BLOCK : BLOCK + 1] + wides[k, u, BLOCK + 1 : BLOCK + 2]
            mixed_of.append(jnp.concatenate(mixed, axis=0) + skip * xs.astype(f32))

        arrived = []
        for i, u in enumerate(gang):
            fall_one, fall_two = falls[i]
            fall = fall_one * fall_two
            sides = []

            @pl.when(has_left)
            def _(u=u):
                state_copy(k, u, 0).wait_recv()

            for side in range(2):
                here = slice(side * BLOCK, (side + 1) * BLOCK)
                incoming = state_in[k, u, side].astype(f32)
                state_out[k, u, side] = (fall[:, here] * incoming + locals_all[i][:, here]).astype(
                    bf16
                )
                sides.append(incoming)

            @pl.when(has_right)
            def _(u=u):
                state_copy(k, u).start()

            arrived.append(jnp.concatenate(sides, axis=1))

        for i, u in enumerate(gang):
            incoming = arrived[i]
            between = (falls[i][0] * incoming + locals_one[i]).astype(bf16)
            off = jnp.concatenate(
                [
                    jnp.dot(c_rows[k, u, :HALF], incoming.astype(bf16), preferred_element_type=f32),
                    jnp.dot(c_rows[k, u, HALF:], between, preferred_element_type=f32),
                ],
                axis=0,
            )
            mixed = mixed_of[i] + off * wides[k, u, :BLOCK]
            gated = mixed * opened[i]
            mean = jnp.sum(gated * gated, axis=1, keepdims=True) * (1.0 / WIDTH)
            result = (
                gated * lax.rsqrt(mean + norm_eps) * gain_buf[k, 0:1, lanes_of(u)]
            ).astype(bf16)
            flow[k + 1, u] = result

        @pl.when(has_right & (k == 0))
        def _():
            for u in gang:
                edge_out[1, u] = folded(flow[1, u, BLOCK - EDGE :])
                edge_copy(1, u, 1).start()

        @pl.when((k == 1) & has_down)
        def _():
            for u in gang:
                prev_copy(u).start()

        @pl.when(k == core)
        def _():
            for u in gang:
                out_ref[0, s, :, lanes_of(u)] = flow[k + 1, u]

        @pl.when(k != core)
        def _():
            for u in gang:
                out_copy(k, u).start()

    few, even, all_gangs = FEW // GANG, EVEN // GANG, UNITS // GANG

    def step(i, carry):
        k, i = i % 2, i // 2
        later = jnp.maximum(i - few, 0)
        u = GANG * jnp.where(
            core == 0,
            i,
            jnp.where(i < few, even + i, few + later // 2 + even * (1 - later % 2)),
        )
        p = u // 2

        @pl.when((u >= low) & (u < low + many))
        def _():
            @pl.when(first_chip & ((k != core) | ((core == 0) & (p >= 2))) & (u % 2 == 0))
            def _():
                prepare(k, p)

            @pl.when((k != core) & (u % 2 == 0))
            def _():
                swap_wait(1, k, p)

            work(k, u)

        return carry

    lax.fori_loop(0, 2 * (even + core * (all_gangs - even - few)), step, 0)

    for i in range(5):
        part_copy(i, core).wait_send()

    @pl.when(has_right)
    def _():
        for i in range(3):
            head_copy(core, i).wait_send()

    def sent(ref, send, there):
        @pl.when(there)
        def _():
            remote(ref, ref, send, out_recv, other).wait_send()

    for n in sorted({FEW // 2, EVEN // 2, PAIRS - FEW // 2}):
        sent(flow.at[0, pl.ds(0, n)], swap_send.at[0], far_pairs == n)
        sent(flow.at[pl.ds(0, 2), pl.ds(0, 2 * n)], swap_send.at[1], far_pairs == n)
        these = n_pairs == n
        sent(state_out.at[:, pl.ds(0, 2 * n)], state_send, these & has_right)
        sent(edge_out.at[1, pl.ds(0, 2 * n)], edge_send.at[1], these & has_right)
        sent(edge_out.at[0, pl.ds(0, 2 * n)], edge_send.at[0], these & has_right & has_up)
        sent(flow.at[0, pl.ds(0, 2 * n)], prev_send, these & has_down)
        sent(flow.at[0, pl.ds(0, 2 * n)], out_send, these)

        @pl.when(far_pairs == n)
        def _(n=n):
            ref = flow.at[0, pl.ds(0, 2 * n)]
            remote(ref, ref, out_send, out_recv, other).wait_recv()


def solution(mesh):
    stages, ranges = mesh.shape["pipe"] // 2, mesh.shape["ctx"]
    f32, bf16 = jnp.float32, jnp.bfloat16
    vmem = pl.BlockSpec(memory_space=pltpu.VMEM)
    hbm = pl.BlockSpec(memory_space=pltpu.HBM)
    dma = pltpu.SemaphoreType.DMA
    pin = functools.partial(pltpu.with_memory_space_constraint, memory_space=pltpu.HBM)

    def on_device(x, gate, bc, dt, rate, weight, skip, gain):
        channels = x.shape[3] + bc.shape[3]
        return pl.pallas_call(
            functools.partial(kernel, stages, ranges),
            out_shape=jax.ShapeDtypeStruct(x.shape, bf16),
            in_specs=[hbm] * 8,
            out_specs=vmem,
            scratch_shapes=[
                pltpu.VMEM((1, SEQS, HEADS, BLOCK), f32),
                pltpu.VMEM(rate.shape, f32),
                pltpu.VMEM(skip.shape, f32),
                pltpu.VMEM((2,) + weight.shape[1:], f32),
                pltpu.VMEM((2,) + gain.shape, f32),
                pltpu.VMEM((2,) + x.shape[1:], bf16),
                pltpu.VMEM((2,) + gate.shape[1:], bf16),
                pltpu.VMEM((2,) + bc.shape[1:], bf16),
                pltpu.VMEM((2, UNITS // 4, BLOCK, BLOCK), bf16),
                pltpu.VMEM((2, BLOCK, PER_GROUP * HALF), bf16),
                pltpu.VMEM((2, ROWS, BLOCK), bf16),
                pltpu.VMEM((BLOCK, BLOCK), f32),
                pltpu.VMEM((3 * 32, PER_GROUP * HALF), bf16),
                pltpu.VMEM((HALF, PER_GROUP * HALF), bf16),
                pltpu.VMEM((2 * BLOCK, 2 * WIDTH), bf16),
                pltpu.VMEM((2, UNITS, BLOCK, PER_GROUP * HALF), bf16),
                pltpu.VMEM((2, UNITS, 2, STATE, HALF), bf16),
                pltpu.VMEM((2, UNITS, BLOCK, STATE), bf16),
                pltpu.VMEM((2, UNITS, BLOCK + EDGE, WIDTH), f32),
                pltpu.VMEM((2, UNITS, BLOCK, WIDTH), bf16),
                pltpu.VMEM((GANG, BLOCK, WIDTH), f32),
                pltpu.VMEM((2 * GANG, PAD + BLOCK, BLOCK), f32),
                pltpu.VMEM((2, PAD + BLOCK, 2 * STATE), f32),
                pltpu.VMEM((SEQS, EDGE, FOLD), bf16),
                pltpu.VMEM((2, SEQS, EDGE, FOLD), bf16),
                pltpu.VMEM((2, SEQS * PAD, channels), f32),
                pltpu.VMEM((3, UNITS, BLOCK, WIDTH), bf16),
                pltpu.VMEM((2, UNITS, PAD, BLOCK), f32),
                pltpu.VMEM((2, UNITS, PAD, BLOCK), f32),
                pltpu.VMEM((2, UNITS, 2, STATE, BLOCK), bf16),
                pltpu.VMEM((2, UNITS, 2, STATE, BLOCK), bf16),
                dma((8,)),
                dma((5,)),
                dma((5,)),
                dma((2,)),
                dma((2, MOST // 2)),
                dma((3,)),
                dma((2, SEQS)),
                dma(()),
                dma((MOST,)),
                dma((2,)),
                dma((2, MOST)),
                dma(()),
                dma((2, MOST)),
                dma(()),
                dma(()),
            ],
            compiler_params=pltpu.CompilerParams(
                collective_id=0, has_side_effects=True, vmem_limit_bytes=52 * 1024 * 1024
            ),
            name="relay",
        )(*map(pin, (x, gate, bc, jnp.swapaxes(dt, 2, 3), rate, weight, skip, gain)))

    rows = P("pipe", None, "ctx", None)
    in_specs = (rows, rows, rows, rows, P("pipe", None), P("pipe", None, None), P("pipe", None), P("pipe", None))
    return jax.shard_map(on_device, mesh=mesh, in_specs=in_specs, out_specs=rows, check_vma=False)
```

```python
import functools

import jax
import jax.numpy as jnp
from jax import lax
from jax.experimental import pallas as pl
from jax.experimental.pallas import tpu as pltpu
from jax.sharding import PartitionSpec as P

HEADS = 64
HEAD_DIM = 32
GROUPS = 8
STATE = 64
BLOCK = 128
HALF = BLOCK // 2
SEQS = 2
PER_GROUP = HEADS // GROUPS
WIDTH = PER_GROUP * HEAD_DIM
HD = HEADS * HEAD_DIM
UNITS = SEQS * GROUPS
PAIRS = UNITS // 2
EDGE = 16
PAD = 8
KEPT = 4
FOLD = (HD + 2 * GROUPS * STATE) * KEPT // EDGE
TAPS = 4
GANG = 1
FEW = 6
EVEN = 8
MOST = max(EVEN, UNITS - FEW)
ROWS = 2 * BLOCK + EDGE

norm_eps = 1e-05
MESH = pl.DeviceIdType.MESH
HIGHEST = lax.Precision.HIGHEST
LOG2E = 1.4426950408889634


def silu_of_twice(half):
    return half * jnp.tanh(half) + half


def conv(buf, weight):
    first = PAD - TAPS + 1
    halves = 0.5 * weight
    total = halves[0:1] * buf[first : first + BLOCK]
    for tap in range(1, TAPS):
        total = total + halves[tap : tap + 1] * buf[first + tap : first + tap + BLOCK]
    return silu_of_twice(total)


def pieces(v):
    parts = []
    for _ in range(3):
        part = v.astype(jnp.bfloat16).astype(jnp.float32)
        parts.append(part)
        v = v - part
    return parts


def kernel(
    stages,
    ranges,
    x_hbm,
    gate_hbm,
    bc_hbm,
    dt_hbm,
    rate_hbm,
    w_hbm,
    skip_hbm,
    gain_hbm,
    out_ref,
    dt_ref,
    rate_ref,
    skip_ref,
    w_buf,
    gain_buf,
    x_buf,
    gate_buf,
    bc_buf,
    lead_buf,
    key_buf,
    pair_buf,
    keys,
    chosen,
    masked,
    shifted,
    weights,
    b_rows,
    c_rows,
    wides,
    tails,
    opened,
    cbuf,
    bbuf,
    head_out,
    head_in,
    heads,
    flow,
    edge,
    edge_out,
    state_in,
    state_out,
    fetch_sem,
    part_send,
    part_recv,
    swap_send,
    swap_recv,
    head_send,
    head_recv,
    prev_send,
    prev_recv,
    edge_send,
    edge_recv,
    state_send,
    state_recv,
    out_send,
    out_recv,
):
    f32, bf16 = jnp.float32, jnp.bfloat16
    section = lax.axis_index("pipe")
    mine = lax.axis_index("ctx")
    stage, core = section // 2, section % 2
    other = 2 * stage + 1 - core
    has_down = stage < stages - 1
    has_up = stage > 0
    has_right = mine < ranges - 1
    has_left = mine > 0
    first_chip = (stage == 0) & (mine == 0)

    def share(at_stage, at_range):
        return jnp.maximum(FEW, EVEN - (EVEN - FEW) * (at_range // 2))

    def owner(u, at_stage, at_range):
        return 2 * at_stage + (u >= share(at_stage, at_range)).astype(jnp.int32)

    def place(u, at_stage, at_range):
        most = share(at_stage, at_range)
        return u - most * (u >= most).astype(jnp.int32)

    shared = share(stage, mine)
    low = core * shared
    many = shared + core * (UNITS - 2 * shared)
    first_pair, n_pairs = low // 2, many // 2
    far_pair, far_pairs = (1 - core) * (shared // 2), PAIRS - n_pairs

    fetches = [
        pltpu.make_async_copy(src, dst, fetch_sem.at[i])
        for i, (src, dst) in enumerate(
            (
                (dt_hbm, dt_ref),
                (rate_hbm, rate_ref),
                (skip_hbm, skip_ref),
                (bc_hbm.at[0], bc_buf.at[core]),
                (x_hbm.at[0], x_buf.at[core]),
                (w_hbm.at[0], w_buf.at[core]),
                (gain_hbm, gain_buf.at[core]),
                (gate_hbm.at[0], gate_buf.at[core]),
            )
        )
    ]
    for fetch in fetches:
        fetch.start()

    barrier = pltpu.get_barrier_semaphore()
    partners = [(core >= 0, other, 0)]
    for there, down, along in (
        (has_right, 0, 1),
        (has_left, 0, -1),
        (has_down, 1, 0),
        (has_up, -1, 0),
    ):
        for side in range(2):
            partners.append((there, 2 * (stage + down) + side, along))
    count = 0
    for there, to, along in partners:
        count = count + there.astype(jnp.int32)

        @pl.when(there)
        def _(to=to, along=along):
            pl.semaphore_signal(
                barrier,
                inc=1,
                device_id={"pipe": to, "ctx": mine + along},
                device_id_type=MESH,
            )

    def remote(src, dst, send, recv, to, along=0):
        return pltpu.make_async_remote_copy(
            src_ref=src,
            dst_ref=dst,
            send_sem=send,
            recv_sem=recv,
            device_id={"pipe": to, "ctx": mine + along},
            device_id_type=MESH,
        )

    def part_copy(i, k):
        src, dst = (
            (lead_buf.at[k], lead_buf),
            (key_buf.at[k], key_buf),
            (pair_buf.at[k], pair_buf),
            (w_hbm.at[0], w_buf),
            (gain_hbm, gain_buf),
        )[i]
        return remote(src, dst.at[k], part_send.at[i], part_recv.at[i], other)

    def swap_copy(kind, k, p, first):
        s, at = p // (GROUPS // 2), p % (GROUPS // 2)
        if kind < 2:
            lanes = pl.ds(pl.multiple_of(kind * GROUPS * STATE + at * 2 * STATE, 2 * STATE), 2 * STATE)
            src, dst = bc_hbm, bc_buf
        else:
            lanes = pl.ds(pl.multiple_of(at * 2 * WIDTH, 2 * WIDTH), 2 * WIDTH)
            src, dst = ((x_hbm, x_buf), (gate_hbm, gate_buf))[kind - 2]
        return remote(
            src.at[0, s, :, lanes],
            dst.at[k, s, :, lanes],
            swap_send.at[kind // 2],
            swap_recv.at[kind // 2, p - first],
            other,
        )

    def swap_wait(half, k, p):
        ref = (bc_buf.at[k, 0, :, pl.ds(0, 4 * STATE)], x_buf.at[k, 0, :, pl.ds(0, 4 * WIDTH)])[half]
        remote(ref, ref, swap_send.at[half], swap_recv.at[half, p - first_pair], other).wait_recv()

    HEAD_PARTS = ((0, 0), (0, 1), (1, 1))

    def head_copy(k, i):
        s, side = HEAD_PARTS[i]
        return remote(
            head_out.at[s],
            head_in.at[k, s],
            head_send.at[i],
            head_recv.at[k, s],
            2 * stage + side,
            1,
        )

    def prev_copy(u, down=1):
        return remote(
            flow.at[2, u],
            flow.at[0, u],
            prev_send,
            prev_recv.at[place(u, stage + down, mine)],
            owner(u, stage + 1, mine),
        )

    def edge_copy(k, u, along=0):
        return remote(
            edge_out.at[k, u],
            edge.at[k, u],
            edge_send.at[k],
            edge_recv.at[k, place(u, stage, mine + along)],
            owner(u, stage, mine + 1),
            1,
        )

    def state_copy(k, u, along=1):
        return remote(
            state_out.at[k, u],
            state_in.at[k, u],
            state_send,
            state_recv.at[k, place(u, stage, mine + along)],
            owner(u, stage, mine + 1),
            1,
        )

    def out_copy(k, u):
        lanes = pl.ds(pl.multiple_of((u % GROUPS) * WIDTH, WIDTH), WIDTH)
        return remote(
            flow.at[k + 1, u],
            out_ref.at[0, u // GROUPS, :, lanes],
            out_send,
            out_recv,
            other,
        )

    sh_rows = lax.broadcasted_iota(jnp.int32, (2 * BLOCK, 2 * WIDTH), 0)
    sh_cols = lax.broadcasted_iota(jnp.int32, (2 * BLOCK, 2 * WIDTH), 1)
    shifted[...] = (sh_rows == BLOCK + sh_cols // HEAD_DIM).astype(bf16)
    ch_rows = lax.broadcasted_iota(jnp.int32, (3 * 32, PER_GROUP * HALF), 0)
    ch_cols = lax.broadcasted_iota(jnp.int32, (3 * 32, PER_GROUP * HALF), 1)
    chosen[...] = (ch_rows % PER_GROUP == ch_cols // HALF).astype(bf16)
    masked[...] = jnp.where(ch_rows[:HALF] < ch_cols[:HALF] % HALF, -1e30, 0.0).astype(bf16)

    for fetch in fetches[:3]:
        fetch.wait()
    rows = lax.broadcasted_iota(jnp.int32, (BLOCK, BLOCK), 0)
    cols = lax.broadcasted_iota(jnp.int32, (BLOCK, BLOCK), 1)
    raw = jnp.concatenate([dt_ref[0, s] for s in range(SEQS)], axis=0)
    steps = jnp.maximum(raw, 0.0) + jnp.log1p(jnp.exp(-jnp.abs(raw)))
    rates = jnp.concatenate([rate_ref[...]] * SEQS, axis=1)
    rates = jnp.broadcast_to(rates, (BLOCK, SEQS * HEADS)).T
    summed = jnp.dot(
        -steps * rates,
        (rows <= cols).astype(f32),
        precision=HIGHEST,
        preferred_element_type=f32,
    )
    keys[...] = summed * LOG2E - jnp.log2(steps)
    left = cols < HALF
    one_keys, two_keys = [], []
    for q in range(PER_GROUP // 2):
        one = keys[pl.ds(2 * q, UNITS, stride=PER_GROUP), :]
        two = keys[pl.ds(2 * q + 1, UNITS, stride=PER_GROUP), :]
        one_keys.append(jnp.where(left[:UNITS], one, pltpu.roll(two, HALF, 1)))
        two_keys.append(jnp.where(left[:UNITS], pltpu.roll(one, HALF, 1), two))
    stacked = jnp.concatenate(
        pieces(jnp.concatenate(one_keys, axis=1)) + pieces(jnp.concatenate(two_keys, axis=1)), axis=0
    ).astype(bf16)
    order = ((cols // UNITS == rows % PER_GROUP) & (cols % UNITS == rows // PER_GROUP))[:, : 6 * UNITS]
    key_buf[core] = jnp.dot(
        order.astype(bf16), stacked, preferred_element_type=f32
    ).astype(bf16)
    cum = summed.T
    slot = cols % PER_GROUP
    halves = jnp.where((slot < 6) & (slot // 3 == rows // HALF), -1.0, 0.0)
    leads = pieces(cum * LOG2E)
    for quad in range(UNITS // 4):
        lead = halves
        for i in (2, 1, 0):
            turn = (32 * (i - quad)) % BLOCK
            part = pltpu.roll(leads[i], turn, 1) if turn else leads[i]
            lead = jnp.where(cols < 32 * (i + 1), part, lead)
        lead_buf[core, quad] = lead.astype(bf16)
    middle, end = cum[HALF - 1 : HALF], cum[BLOCK - 1 : BLOCK]
    grown = jnp.exp(jnp.where(rows < HALF, cum, cum - middle))
    tail = jnp.exp(jnp.where(rows < HALF, middle, end) - cum) * steps.T
    skips = jnp.concatenate([skip_ref[...]] * SEQS, axis=1)
    extra = jnp.zeros((EDGE, BLOCK), f32)
    slot = rows[:EDGE]
    for i, row in enumerate((skips, grown[HALF - 1 : HALF], grown[BLOCK - 1 : BLOCK])):
        row_high = row.astype(bf16).astype(f32)
        extra = jnp.where(slot == 2 * i, row_high, extra)
        extra = jnp.where(slot == 2 * i + 1, row - row_high, extra)
    pair_buf[core] = jnp.concatenate([grown, extra, tail], axis=0).astype(bf16)

    fetches[3].wait()
    fetches[4].wait()
    for s in range(SEQS):
        last = jnp.concatenate(
            [
                ref[core, s, BLOCK - EDGE :, :].astype(f32)[EDGE - KEPT :]
                for ref in (x_buf, bc_buf)
            ],
            axis=1,
        )
        head_out[s] = jnp.concatenate(
            [last[:, m * FOLD : (m + 1) * FOLD] for m in range(EDGE // KEPT)], axis=0
        ).astype(bf16)
    pl.semaphore_wait(barrier, count)

    @pl.when(has_right)
    def _():
        for i in range(3):
            head_copy(core, i).start()

    for i in range(4):
        part_copy(i, core).start()

    def swap(p, carry):
        for kind in range(4):
            swap_copy(kind, core, p, far_pair).start()
        return carry

    lax.fori_loop(far_pair, far_pair + far_pairs, swap, 0)
    part_copy(4, core).start()

    @pl.when(jnp.logical_not(has_left))
    def _():
        heads[...] = jnp.zeros_like(heads)

    @pl.when(has_left)
    def _():
        def unfold(k, s):
            folded = head_in[k, s].astype(f32)
            for m in range(EDGE // KEPT):
                heads[k, s * PAD + PAD - KEPT : (s + 1) * PAD, m * FOLD : (m + 1) * FOLD] = folded[
                    m * KEPT : (m + 1) * KEPT
                ]

        for k in range(2):
            head_copy(k, 0).wait_recv()
            unfold(k, 0)

            @pl.when(core == 1)
            def _(k=k):
                head_copy(k, 2).wait_recv()
                unfold(k, 1)

    fetches[5].wait()
    left = left[:HALF]
    unit_of = cols % 32 // PER_GROUP
    token_of = (rows % HALF == cols)[:, :HALF].astype(bf16)

    def prepare(k, p):
        @pl.when(k != core)
        def _():
            @pl.when(p == first_pair)
            def _():
                for i in range(5):
                    part_copy(i, k).wait_recv()

            swap_wait(0, k, p)

        s, pair = p // (GROUPS // 2), p % (GROUPS // 2)
        acts = []
        for part in range(2):
            at = pl.multiple_of(part * GROUPS * STATE + pair * 2 * STATE, 2 * STATE)
            wide = pl.ds(pl.multiple_of(HD + at, 2 * STATE), 2 * STATE)
            bbuf[part, pl.ds(0, PAD), :] = heads[k, pl.ds(pl.multiple_of(s * PAD, PAD), PAD), wide]
            bbuf[part, pl.ds(PAD, BLOCK), :] = bc_buf[k, s, :, pl.ds(at, 2 * STATE)].astype(f32)
            acts.append(conv(bbuf.at[part], w_buf[k, :, wide]).astype(bf16))
        b_t = acts[0].astype(f32).T
        quad = p // 2
        lead = lead_buf[k, quad]
        chooser = jnp.concatenate(
            [chosen[...], key_buf[k, pl.ds(pl.multiple_of(quad * 32, 32), 32), :], masked[...]], axis=0
        )
        lead_rows = [
            jnp.where(unit_of == (2 * p + half) % 4, lead, jnp.zeros_like(lead)) for half in range(2)
        ]
        gap = jnp.dot(
            jnp.concatenate(
                [jnp.concatenate(lead_rows, axis=0), jnp.concatenate([token_of] * 2, axis=0)], axis=1
            ),
            chooser,
            preferred_element_type=f32,
        )
        spread = shifted[pl.ds(pl.multiple_of(BLOCK - 2 * PER_GROUP * p, 2 * PER_GROUP), BLOCK), :]
        wide = jnp.dot(pair_buf[k], spread, preferred_element_type=f32)
        for half in range(2):
            u = 2 * p + half
            c_u = acts[1][:, half * STATE : (half + 1) * STATE]
            b_u = b_t[half * STATE : (half + 1) * STATE]
            b_turned = pltpu.roll(b_u, HALF, 1)
            b_one = jnp.where(left, b_u, b_turned).astype(bf16)
            b_two = jnp.where(left, b_turned, b_u).astype(bf16)
            c_rows[k, u] = c_u
            b_rows[k, u, 0] = b_one[:, :HALF]
            b_rows[k, u, 1] = b_two[:, :HALF]
            scores = (
                jnp.dot(c_u[:HALF], b_one, preferred_element_type=f32),
                jnp.dot(c_u[HALF:], b_two, preferred_element_type=f32),
            )
            for part in range(2):
                tokens = slice(part * HALF, (part + 1) * HALF)
                gap_rows = slice((2 * half + part) * HALF, (2 * half + part + 1) * HALF)
                for q in range(PER_GROUP // 2):
                    lanes = slice(q * BLOCK, (q + 1) * BLOCK)
                    weights[k, u, tokens, lanes] = (
                        scores[part] * jnp.exp2(gap[gap_rows, lanes])
                    ).astype(bf16)
            here = slice(half * WIDTH, (half + 1) * WIDTH)
            wides[k, u] = wide[: BLOCK + EDGE, here]
            tails[k, u] = wide[BLOCK + EDGE :, here].astype(bf16)

    def ahead(i, carry):
        turn = i // n_pairs
        k = core + turn * (1 - 2 * core)
        prepare(k, first_pair + i % n_pairs)
        return carry

    lazy = first_chip.astype(jnp.int32)
    lax.fori_loop(0, n_pairs * (2 - lazy) - lazy * (1 - core) * (n_pairs - 2), ahead, 0)

    fetches[6].wait()
    fetches[7].wait()
    lane_head = lax.broadcasted_iota(jnp.int32, (HALF, BLOCK), 1) // HEAD_DIM

    def folded(tail):
        last = tail.astype(f32)[EDGE - KEPT :]
        return jnp.concatenate([last[:, :BLOCK], last[:, BLOCK:]], axis=0)

    def work(k, first):
        s = first // GROUPS
        gang = tuple(first + i for i in range(GANG))

        def lanes_of(u, side=0, width=WIDTH):
            return pl.ds(pl.multiple_of((u % GROUPS) * WIDTH + side * width, width), width)

        @pl.when((k == 0) & jnp.logical_not(has_up))
        def _():
            for u in gang:
                flow[0, u] = jnp.zeros(flow.shape[2:], bf16)

        @pl.when(jnp.logical_not(has_left & ((k == 1) | has_up)))
        def _():
            for u in gang:
                edge[k, u] = jnp.zeros(edge.shape[2:], f32)

        @pl.when(jnp.logical_not(has_left))
        def _():
            for u in gang:
                state_in[k, u] = jnp.zeros(state_in.shape[2:], bf16)

        xs_of, falls, locals_one, locals_all, mixed_of = [], [], [], [], []
        for i, u in enumerate(gang):
            gate = (0.5 * gate_buf[k, s, :, lanes_of(u)]).astype(f32)
            opened[i] = silu_of_twice(gate)
        for i, u in enumerate(gang):
            sides = []
            @pl.when((k == 0) & has_up)
            def _(u=u):
                prev_copy(u, 0).wait_recv()

            @pl.when((k == 0) & has_up & has_right)
            def _(u=u):
                edge_out[0, u] = folded(flow[0, u, BLOCK - EDGE :])
                edge_copy(0, u, 1).start()

            @pl.when(has_left & ((k == 1) | has_up))
            def _(u=u):
                edge_copy(k, u).wait_recv()

            for side in range(2):
                at = lanes_of(u, side, BLOCK)
                buf = cbuf.at[2 * i + side]
                buf[pl.ds(0, PAD), :] = heads[k, pl.ds(pl.multiple_of(s * PAD, PAD), PAD), at]
                buf[pl.ds(PAD - KEPT, KEPT), :] += edge[k, u, side * KEPT : (side + 1) * KEPT]
                buf[pl.ds(PAD, BLOCK), :] = x_buf[k, s, :, at].astype(f32) + flow[
                    k, u, :, side * BLOCK : (side + 1) * BLOCK
                ].astype(f32)
                sides.append(conv(buf, w_buf[k, :, at]).astype(bf16))
            xs = jnp.concatenate(sides, axis=1)
            xs_of.append(xs)
            keyed = xs * tails[k, u]
            extra = wides[k, u, BLOCK : BLOCK + PAD]
            fall_one, fall_two = extra[2:3] + extra[3:4], extra[4:5] + extra[5:6]
            local_one = jnp.dot(b_rows[k, u, 0], keyed[:HALF], preferred_element_type=f32)
            local_two = jnp.dot(b_rows[k, u, 1], keyed[HALF:], preferred_element_type=f32)
            falls.append((fall_one, fall_two))
            locals_one.append(local_one)
            locals_all.append(fall_two * local_one + local_two)
        zero = jnp.zeros((HALF, BLOCK), bf16)
        for u, xs in zip(gang, xs_of):
            mixed = []
            for part in range(2):
                tokens = slice(part * HALF, (part + 1) * HALF)
                sides = []
                for side in range(2):
                    xs_side = xs[tokens, side * BLOCK : (side + 1) * BLOCK]
                    diagonal = jnp.concatenate(
                        [jnp.where(lane_head == h, xs_side, zero) for h in range(PER_GROUP // 2)],
                        axis=0,
                    )
                    sides.append(
                        jnp.dot(
                            weights[k, u, tokens, side * WIDTH : (side + 1) * WIDTH],
                            diagonal,
                            preferred_element_type=f32,
                        )
                    )
                mixed.append(jnp.concatenate(sides, axis=1))
            skip = wides[k, u, BLOCK : BLOCK + 1] + wides[k, u, BLOCK + 1 : BLOCK + 2]
            mixed_of.append(jnp.concatenate(mixed, axis=0) + skip * xs.astype(f32))

        arrived = []
        for i, u in enumerate(gang):
            fall_one, fall_two = falls[i]
            fall = fall_one * fall_two
            sides = []

            @pl.when(has_left)
            def _(u=u):
                state_copy(k, u, 0).wait_recv()

            for side in range(2):
                here = slice(side * BLOCK, (side + 1) * BLOCK)
                incoming = state_in[k, u, side].astype(f32)
                state_out[k, u, side] = (fall[:, here] * incoming + locals_all[i][:, here]).astype(
                    bf16
                )
                sides.append(incoming)

            @pl.when(has_right)
            def _(u=u):
                state_copy(k, u).start()

            arrived.append(jnp.concatenate(sides, axis=1))

        for i, u in enumerate(gang):
            incoming = arrived[i]
            between = (falls[i][0] * incoming + locals_one[i]).astype(bf16)
            off = jnp.concatenate(
                [
                    jnp.dot(c_rows[k, u, :HALF], incoming.astype(bf16), preferred_element_type=f32),
                    jnp.dot(c_rows[k, u, HALF:], between, preferred_element_type=f32),
                ],
                axis=0,
            )
            mixed = mixed_of[i] + off * wides[k, u, :BLOCK]
            gated = mixed * opened[i]
            mean = jnp.sum(gated * gated, axis=1, keepdims=True) * (1.0 / WIDTH)
            result = (
                gated * lax.rsqrt(mean + norm_eps) * gain_buf[k, 0:1, lanes_of(u)]
            ).astype(bf16)
            flow[k + 1, u] = result

        @pl.when(has_right & (k == 0))
        def _():
            for u in gang:
                edge_out[1, u] = folded(flow[1, u, BLOCK - EDGE :])
                edge_copy(1, u, 1).start()

        @pl.when((k == 1) & has_down)
        def _():
            for u in gang:
                prev_copy(u).start()

        @pl.when(k == core)
        def _():
            for u in gang:
                out_ref[0, s, :, lanes_of(u)] = flow[k + 1, u]

        @pl.when(k != core)
        def _():
            for u in gang:
                out_copy(k, u).start()

    few, even, all_gangs = FEW // GANG, EVEN // GANG, UNITS // GANG

    def step(i, carry):
        k, i = i % 2, i // 2
        later = jnp.maximum(i - few, 0)
        u = GANG * jnp.where(
            core == 0,
            i,
            jnp.where(i < few, even + i, few + later // 2 + even * (1 - later % 2)),
        )
        p = u // 2

        @pl.when((u >= low) & (u < low + many))
        def _():
            @pl.when(first_chip & ((k != core) | ((core == 0) & (p >= 2))) & (u % 2 == 0))
            def _():
                prepare(k, p)

            @pl.when((k != core) & (u % 2 == 0))
            def _():
                swap_wait(1, k, p)

            work(k, u)

        return carry

    lax.fori_loop(0, 2 * (even + core * (all_gangs - even - few)), step, 0)

    for i in range(5):
        part_copy(i, core).wait_send()

    @pl.when(has_right)
    def _():
        for i in range(3):
            head_copy(core, i).wait_send()

    def sent(ref, send, there):
        @pl.when(there)
        def _():
            remote(ref, ref, send, out_recv, other).wait_send()

    for n in sorted({FEW // 2, EVEN // 2, PAIRS - FEW // 2}):
        sent(flow.at[0, pl.ds(0, n)], swap_send.at[0], far_pairs == n)
        sent(flow.at[pl.ds(0, 2), pl.ds(0, 2 * n)], swap_send.at[1], far_pairs == n)
        these = n_pairs == n
        sent(state_out.at[:, pl.ds(0, 2 * n)], state_send, these & has_right)
        sent(edge_out.at[1, pl.ds(0, 2 * n)], edge_send.at[1], these & has_right)
        sent(edge_out.at[0, pl.ds(0, 2 * n)], edge_send.at[0], these & has_right & has_up)
        sent(flow.at[0, pl.ds(0, 2 * n)], prev_send, these & has_down)
        sent(flow.at[0, pl.ds(0, 2 * n)], out_send, these)

        @pl.when(far_pairs == n)
        def _(n=n):
            ref = flow.at[0, pl.ds(0, 2 * n)]
            remote(ref, ref, out_send, out_recv, other).wait_recv()


def solution(mesh):
    stages, ranges = mesh.shape["pipe"] // 2, mesh.shape["ctx"]
    f32, bf16 = jnp.float32, jnp.bfloat16
    vmem = pl.BlockSpec(memory_space=pltpu.VMEM)
    hbm = pl.BlockSpec(memory_space=pltpu.HBM)
    dma = pltpu.SemaphoreType.DMA
    pin = functools.partial(pltpu.with_memory_space_constraint, memory_space=pltpu.HBM)

    def on_device(x, gate, bc, dt, rate, weight, skip, gain):
        channels = x.shape[3] + bc.shape[3]
        return pl.pallas_call(
            functools.partial(kernel, stages, ranges),
            out_shape=jax.ShapeDtypeStruct(x.shape, bf16),
            in_specs=[hbm] * 8,
            out_specs=vmem,
            scratch_shapes=[
                pltpu.VMEM((1, SEQS, HEADS, BLOCK), f32),
                pltpu.VMEM(rate.shape, f32),
                pltpu.VMEM(skip.shape, f32),
                pltpu.VMEM((2,) + weight.shape[1:], f32),
                pltpu.VMEM((2,) + gain.shape, f32),
                pltpu.VMEM((2,) + x.shape[1:], bf16),
                pltpu.VMEM((2,) + gate.shape[1:], bf16),
                pltpu.VMEM((2,) + bc.shape[1:], bf16),
                pltpu.VMEM((2, UNITS // 4, BLOCK, BLOCK), bf16),
                pltpu.VMEM((2, BLOCK, PER_GROUP * HALF), bf16),
                pltpu.VMEM((2, ROWS, BLOCK), bf16),
                pltpu.VMEM((BLOCK, BLOCK), f32),
                pltpu.VMEM((3 * 32, PER_GROUP * HALF), bf16),
                pltpu.VMEM((HALF, PER_GROUP * HALF), bf16),
                pltpu.VMEM((2 * BLOCK, 2 * WIDTH), bf16),
                pltpu.VMEM((2, UNITS, BLOCK, PER_GROUP * HALF), bf16),
                pltpu.VMEM((2, UNITS, 2, STATE, HALF), bf16),
                pltpu.VMEM((2, UNITS, BLOCK, STATE), bf16),
                pltpu.VMEM((2, UNITS, BLOCK + EDGE, WIDTH), f32),
                pltpu.VMEM((2, UNITS, BLOCK, WIDTH), bf16),
                pltpu.VMEM((GANG, BLOCK, WIDTH), f32),
                pltpu.VMEM((2 * GANG, PAD + BLOCK, BLOCK), f32),
                pltpu.VMEM((2, PAD + BLOCK, 2 * STATE), f32),
                pltpu.VMEM((SEQS, EDGE, FOLD), bf16),
                pltpu.VMEM((2, SEQS, EDGE, FOLD), bf16),
                pltpu.VMEM((2, SEQS * PAD, channels), f32),
                pltpu.VMEM((3, UNITS, BLOCK, WIDTH), bf16),
                pltpu.VMEM((2, UNITS, PAD, BLOCK), f32),
                pltpu.VMEM((2, UNITS, PAD, BLOCK), f32),
                pltpu.VMEM((2, UNITS, 2, STATE, BLOCK), bf16),
                pltpu.VMEM((2, UNITS, 2, STATE, BLOCK), bf16),
                dma((8,)),
                dma((5,)),
                dma((5,)),
                dma((2,)),
                dma((2, MOST // 2)),
                dma((3,)),
                dma((2, SEQS)),
                dma(()),
                dma((MOST,)),
                dma((2,)),
                dma((2, MOST)),
                dma(()),
                dma((2, MOST)),
                dma(()),
                dma(()),
            ],
            compiler_params=pltpu.CompilerParams(
                collective_id=0, has_side_effects=True, vmem_limit_bytes=52 * 1024 * 1024
            ),
            name="relay",
        )(*map(pin, (x, gate, bc, jnp.swapaxes(dt, 2, 3), rate, weight, skip, gain)))

    rows = P("pipe", None, "ctx", None)
    in_specs = (rows, rows, rows, rows, P("pipe", None), P("pipe", None, None), P("pipe", None), P("pipe", None))
    return jax.shard_map(on_device, mesh=mesh, in_specs=in_specs, out_specs=rows, check_vma=False)
```

```python
import functools

import jax
import jax.numpy as jnp
from jax import lax
from jax.experimental import pallas as pl
from jax.experimental.pallas import tpu as pltpu
from jax.sharding import PartitionSpec as P

HEADS = 64
HEAD_DIM = 32
GROUPS = 8
STATE = 64
BLOCK = 128
HALF = BLOCK // 2
SEQS = 2
PER_GROUP = HEADS // GROUPS
WIDTH = PER_GROUP * HEAD_DIM
HD = HEADS * HEAD_DIM
UNITS = SEQS * GROUPS
PAIRS = UNITS // 2
EDGE = 16
PAD = 8
KEPT = 4
FOLD = (HD + 2 * GROUPS * STATE) * KEPT // EDGE
TAPS = 4
GANG = 1
FEW = 6
EVEN = 8
MOST = max(EVEN, UNITS - FEW)
ROWS = 2 * BLOCK + EDGE

norm_eps = 1e-05
MESH = pl.DeviceIdType.MESH
HIGHEST = lax.Precision.HIGHEST
LOG2E = 1.4426950408889634


def silu_of_twice(half):
    return half * jnp.tanh(half) + half


def conv(buf, weight):
    first = PAD - TAPS + 1
    halves = 0.5 * weight
    total = halves[0:1] * buf[first : first + BLOCK]
    for tap in range(1, TAPS):
        total = total + halves[tap : tap + 1] * buf[first + tap : first + tap + BLOCK]
    return silu_of_twice(total)


def pieces(v):
    parts = []
    for _ in range(3):
        part = v.astype(jnp.bfloat16).astype(jnp.float32)
        parts.append(part)
        v = v - part
    return parts


def kernel(
    stages,
    ranges,
    x_hbm,
    gate_hbm,
    bc_hbm,
    dt_hbm,
    rate_hbm,
    w_hbm,
    skip_hbm,
    gain_hbm,
    out_ref,
    dt_ref,
    rate_ref,
    skip_ref,
    w_buf,
    gain_buf,
    x_buf,
    gate_buf,
    bc_buf,
    lead_buf,
    key_buf,
    pair_buf,
    keys,
    chosen,
    masked,
    shifted,
    weights,
    b_rows,
    c_rows,
    wides,
    tails,
    opened,
    cbuf,
    bbuf,
    head_out,
    head_in,
    heads,
    flow,
    edge,
    edge_out,
    state_in,
    state_out,
    fetch_sem,
    part_send,
    part_recv,
    swap_send,
    swap_recv,
    head_send,
    head_recv,
    prev_send,
    prev_recv,
    edge_send,
    edge_recv,
    state_send,
    state_recv,
    out_send,
    out_recv,
):
    f32, bf16 = jnp.float32, jnp.bfloat16
    section = lax.axis_index("pipe")
    mine = lax.axis_index("ctx")
    stage, core = section // 2, section % 2
    other = 2 * stage + 1 - core
    has_down = stage < stages - 1
    has_up = stage > 0
    has_right = mine < ranges - 1
    has_left = mine > 0
    first_chip = (stage == 0) & (mine == 0)

    def share(at_stage, at_range):
        return jnp.maximum(FEW, EVEN - (EVEN - FEW) * (at_range // 2))

    def owner(u, at_stage, at_range):
        return 2 * at_stage + (u >= share(at_stage, at_range)).astype(jnp.int32)

    def place(u, at_stage, at_range):
        most = share(at_stage, at_range)
        return u - most * (u >= most).astype(jnp.int32)

    shared = share(stage, mine)
    low = core * shared
    many = shared + core * (UNITS - 2 * shared)
    first_pair, n_pairs = low // 2, many // 2
    far_pair, far_pairs = (1 - core) * (shared // 2), PAIRS - n_pairs

    fetches = [
        pltpu.make_async_copy(src, dst, fetch_sem.at[i])
        for i, (src, dst) in enumerate(
            (
                (dt_hbm, dt_ref),
                (rate_hbm, rate_ref),
                (skip_hbm, skip_ref),
                (bc_hbm.at[0], bc_buf.at[core]),
                (x_hbm.at[0], x_buf.at[core]),
                (w_hbm.at[0], w_buf.at[core]),
                (gain_hbm, gain_buf.at[core]),
                (gate_hbm.at[0], gate_buf.at[core]),
            )
        )
    ]
    barrier = pltpu.get_barrier_semaphore()
    partners = [(core >= 0, other, 0)]
    for there, down, along in (
        (has_right, 0, 1),
        (has_left, 0, -1),
        (has_down, 1, 0),
        (has_up, -1, 0),
    ):
        for side in range(2):
            partners.append((there, 2 * (stage + down) + side, along))
    count = 0
    for there, to, along in partners:
        count = count + there.astype(jnp.int32)

        @pl.when(there)
        def _(to=to, along=along):
            pl.semaphore_signal(
                barrier,
                inc=1,
                device_id={"pipe": to, "ctx": mine + along},
                device_id_type=MESH,
            )

    for fetch in fetches:
        fetch.start()

    def remote(src, dst, send, recv, to, along=0):
        return pltpu.make_async_remote_copy(
            src_ref=src,
            dst_ref=dst,
            send_sem=send,
            recv_sem=recv,
            device_id={"pipe": to, "ctx": mine + along},
            device_id_type=MESH,
        )

    def part_copy(i, k):
        src, dst = (
            (lead_buf.at[k], lead_buf),
            (key_buf.at[k], key_buf),
            (pair_buf.at[k], pair_buf),
            (w_hbm.at[0], w_buf),
            (gain_hbm, gain_buf),
        )[i]
        return remote(src, dst.at[k], part_send.at[i], part_recv.at[i], other)

    def swap_copy(kind, k, p, first):
        s, at = p // (GROUPS // 2), p % (GROUPS // 2)
        if kind < 2:
            lanes = pl.ds(pl.multiple_of(kind * GROUPS * STATE + at * 2 * STATE, 2 * STATE), 2 * STATE)
            src, dst = bc_hbm, bc_buf
        else:
            lanes = pl.ds(pl.multiple_of(at * 2 * WIDTH, 2 * WIDTH), 2 * WIDTH)
            src, dst = ((x_hbm, x_buf), (gate_hbm, gate_buf))[kind - 2]
        return remote(
            src.at[0, s, :, lanes],
            dst.at[k, s, :, lanes],
            swap_send.at[kind // 2],
            swap_recv.at[kind // 2, p - first],
            other,
        )

    def swap_wait(half, k, p):
        ref = (bc_buf.at[k, 0, :, pl.ds(0, 4 * STATE)], x_buf.at[k, 0, :, pl.ds(0, 4 * WIDTH)])[half]
        remote(ref, ref, swap_send.at[half], swap_recv.at[half, p - first_pair], other).wait_recv()

    HEAD_PARTS = ((0, 0), (0, 1), (1, 1))

    def head_copy(k, i):
        s, side = HEAD_PARTS[i]
        return remote(
            head_out.at[s],
            head_in.at[k, s],
            head_send.at[i],
            head_recv.at[k, s],
            2 * stage + side,
            1,
        )

    def prev_copy(u, down=1):
        return remote(
            flow.at[2, u],
            flow.at[0, u],
            prev_send,
            prev_recv.at[place(u, stage + down, mine)],
            owner(u, stage + 1, mine),
        )

    def edge_copy(k, u, along=0):
        return remote(
            edge_out.at[k, u],
            edge.at[k, u],
            edge_send.at[k],
            edge_recv.at[k, place(u, stage, mine + along)],
            owner(u, stage, mine + 1),
            1,
        )

    def state_copy(k, u, along=1):
        return remote(
            state_out.at[k, u],
            state_in.at[k, u],
            state_send,
            state_recv.at[k, place(u, stage, mine + along)],
            owner(u, stage, mine + 1),
            1,
        )

    def out_copy(k, u):
        lanes = pl.ds(pl.multiple_of((u % GROUPS) * WIDTH, WIDTH), WIDTH)
        return remote(
            flow.at[k + 1, u],
            out_ref.at[0, u // GROUPS, :, lanes],
            out_send,
            out_recv,
            other,
        )

    sh_rows = lax.broadcasted_iota(jnp.int32, (2 * BLOCK, 2 * WIDTH), 0)
    sh_cols = lax.broadcasted_iota(jnp.int32, (2 * BLOCK, 2 * WIDTH), 1)
    shifted[...] = (sh_rows == BLOCK + sh_cols // HEAD_DIM).astype(bf16)
    ch_rows = lax.broadcasted_iota(jnp.int32, (3 * 32, PER_GROUP * HALF), 0)
    ch_cols = lax.broadcasted_iota(jnp.int32, (3 * 32, PER_GROUP * HALF), 1)
    chosen[...] = (ch_rows % PER_GROUP == ch_cols // HALF).astype(bf16)
    masked[...] = jnp.where(ch_rows[:HALF] < ch_cols[:HALF] % HALF, -1e30, 0.0).astype(bf16)

    for fetch in fetches[:3]:
        fetch.wait()
    rows = lax.broadcasted_iota(jnp.int32, (BLOCK, BLOCK), 0)
    cols = lax.broadcasted_iota(jnp.int32, (BLOCK, BLOCK), 1)
    raw = jnp.concatenate([dt_ref[0, s] for s in range(SEQS)], axis=0)
    steps = jnp.maximum(raw, 0.0) + jnp.log1p(jnp.exp(-jnp.abs(raw)))
    rates = jnp.concatenate([rate_ref[...]] * SEQS, axis=1)
    rates = jnp.broadcast_to(rates, (BLOCK, SEQS * HEADS)).T
    summed = jnp.dot(
        -steps * rates,
        (rows <= cols).astype(f32),
        precision=HIGHEST,
        preferred_element_type=f32,
    )
    keys[...] = summed * LOG2E - jnp.log2(steps)
    left = cols < HALF
    one_keys, two_keys = [], []
    for q in range(PER_GROUP // 2):
        one = keys[pl.ds(2 * q, UNITS, stride=PER_GROUP), :]
        two = keys[pl.ds(2 * q + 1, UNITS, stride=PER_GROUP), :]
        one_keys.append(jnp.where(left[:UNITS], one, pltpu.roll(two, HALF, 1)))
        two_keys.append(jnp.where(left[:UNITS], pltpu.roll(one, HALF, 1), two))
    stacked = jnp.concatenate(
        pieces(jnp.concatenate(one_keys, axis=1)) + pieces(jnp.concatenate(two_keys, axis=1)), axis=0
    ).astype(bf16)
    order = ((cols // UNITS == rows % PER_GROUP) & (cols % UNITS == rows // PER_GROUP))[:, : 6 * UNITS]
    key_buf[core] = jnp.dot(
        order.astype(bf16), stacked, preferred_element_type=f32
    ).astype(bf16)
    cum = summed.T
    slot = cols % PER_GROUP
    halves = jnp.where((slot < 6) & (slot // 3 == rows // HALF), -1.0, 0.0)
    leads = pieces(cum * LOG2E)
    for quad in range(UNITS // 4):
        lead = halves
        for i in (2, 1, 0):
            turn = (32 * (i - quad)) % BLOCK
            part = pltpu.roll(leads[i], turn, 1) if turn else leads[i]
            lead = jnp.where(cols < 32 * (i + 1), part, lead)
        lead_buf[core, quad] = lead.astype(bf16)
    middle, end = cum[HALF - 1 : HALF], cum[BLOCK - 1 : BLOCK]
    grown = jnp.exp(jnp.where(rows < HALF, cum, cum - middle))
    tail = jnp.exp(jnp.where(rows < HALF, middle, end) - cum) * steps.T
    skips = jnp.concatenate([skip_ref[...]] * SEQS, axis=1)
    extra = jnp.zeros((EDGE, BLOCK), f32)
    slot = rows[:EDGE]
    for i, row in enumerate((skips, grown[HALF - 1 : HALF], grown[BLOCK - 1 : BLOCK])):
        row_high = row.astype(bf16).astype(f32)
        extra = jnp.where(slot == 2 * i, row_high, extra)
        extra = jnp.where(slot == 2 * i + 1, row - row_high, extra)
    pair_buf[core] = jnp.concatenate([grown, extra, tail], axis=0).astype(bf16)

    fetches[3].wait()
    fetches[4].wait()
    for s in range(SEQS):
        last = jnp.concatenate(
            [
                ref[core, s, BLOCK - EDGE :, :].astype(f32)[EDGE - KEPT :]
                for ref in (x_buf, bc_buf)
            ],
            axis=1,
        )
        head_out[s] = jnp.concatenate(
            [last[:, m * FOLD : (m + 1) * FOLD] for m in range(EDGE // KEPT)], axis=0
        ).astype(bf16)
    pl.semaphore_wait(barrier, count)

    @pl.when(has_right)
    def _():
        for i in range(3):
            head_copy(core, i).start()

    for i in range(4):
        part_copy(i, core).start()

    def swap(p, carry):
        for kind in range(4):
            swap_copy(kind, core, p, far_pair).start()
        return carry

    lax.fori_loop(far_pair, far_pair + far_pairs, swap, 0)
    part_copy(4, core).start()

    @pl.when(jnp.logical_not(has_left))
    def _():
        heads[...] = jnp.zeros_like(heads)

    @pl.when(has_left)
    def _():
        def unfold(k, s):
            folded = head_in[k, s].astype(f32)
            for m in range(EDGE // KEPT):
                heads[k, s * PAD + PAD - KEPT : (s + 1) * PAD, m * FOLD : (m + 1) * FOLD] = folded[
                    m * KEPT : (m + 1) * KEPT
                ]

        for k in range(2):
            head_copy(k, 0).wait_recv()
            unfold(k, 0)

            @pl.when(core == 1)
            def _(k=k):
                head_copy(k, 2).wait_recv()
                unfold(k, 1)

    fetches[5].wait()
    left = left[:HALF]
    unit_of = cols % 32 // PER_GROUP
    token_of = (rows % HALF == cols)[:, :HALF].astype(bf16)

    def prepare(k, p):
        @pl.when(k != core)
        def _():
            @pl.when(p == first_pair)
            def _():
                for i in range(5):
                    part_copy(i, k).wait_recv()

            swap_wait(0, k, p)

        s, pair = p // (GROUPS // 2), p % (GROUPS // 2)
        acts = []
        for part in range(2):
            at = pl.multiple_of(part * GROUPS * STATE + pair * 2 * STATE, 2 * STATE)
            wide = pl.ds(pl.multiple_of(HD + at, 2 * STATE), 2 * STATE)
            bbuf[part, pl.ds(0, PAD), :] = heads[k, pl.ds(pl.multiple_of(s * PAD, PAD), PAD), wide]
            bbuf[part, pl.ds(PAD, BLOCK), :] = bc_buf[k, s, :, pl.ds(at, 2 * STATE)].astype(f32)
            acts.append(conv(bbuf.at[part], w_buf[k, :, wide]).astype(bf16))
        b_t = acts[0].astype(f32).T
        quad = p // 2
        lead = lead_buf[k, quad]
        chooser = jnp.concatenate(
            [chosen[...], key_buf[k, pl.ds(pl.multiple_of(quad * 32, 32), 32), :], masked[...]], axis=0
        )
        lead_rows = [
            jnp.where(unit_of == (2 * p + half) % 4, lead, jnp.zeros_like(lead)) for half in range(2)
        ]
        gap = jnp.dot(
            jnp.concatenate(
                [jnp.concatenate(lead_rows, axis=0), jnp.concatenate([token_of] * 2, axis=0)], axis=1
            ),
            chooser,
            preferred_element_type=f32,
        )
        spread = shifted[pl.ds(pl.multiple_of(BLOCK - 2 * PER_GROUP * p, 2 * PER_GROUP), BLOCK), :]
        wide = jnp.dot(pair_buf[k], spread, preferred_element_type=f32)
        for half in range(2):
            u = 2 * p + half
            c_u = acts[1][:, half * STATE : (half + 1) * STATE]
            b_u = b_t[half * STATE : (half + 1) * STATE]
            b_turned = pltpu.roll(b_u, HALF, 1)
            b_one = jnp.where(left, b_u, b_turned).astype(bf16)
            b_two = jnp.where(left, b_turned, b_u).astype(bf16)
            c_rows[k, u] = c_u
            b_rows[k, u, 0] = b_one[:, :HALF]
            b_rows[k, u, 1] = b_two[:, :HALF]
            scores = (
                jnp.dot(c_u[:HALF], b_one, preferred_element_type=f32),
                jnp.dot(c_u[HALF:], b_two, preferred_element_type=f32),
            )
            for part in range(2):
                tokens = slice(part * HALF, (part + 1) * HALF)
                gap_rows = slice((2 * half + part) * HALF, (2 * half + part + 1) * HALF)
                for q in range(PER_GROUP // 2):
                    lanes = slice(q * BLOCK, (q + 1) * BLOCK)
                    weights[k, u, tokens, lanes] = (
                        scores[part] * jnp.exp2(gap[gap_rows, lanes])
                    ).astype(bf16)
            here = slice(half * WIDTH, (half + 1) * WIDTH)
            wides[k, u] = wide[: BLOCK + EDGE, here]
            tails[k, u] = wide[BLOCK + EDGE :, here].astype(bf16)

    def ahead(i, carry):
        turn = i // n_pairs
        k = core + turn * (1 - 2 * core)
        prepare(k, first_pair + i % n_pairs)
        return carry

    lazy = first_chip.astype(jnp.int32)
    lax.fori_loop(0, n_pairs * (2 - lazy) - lazy * (1 - core) * (n_pairs - 2), ahead, 0)

    fetches[6].wait()
    fetches[7].wait()
    lane_head = lax.broadcasted_iota(jnp.int32, (HALF, BLOCK), 1) // HEAD_DIM

    def folded(tail):
        last = tail.astype(f32)[EDGE - KEPT :]
        return jnp.concatenate([last[:, :BLOCK], last[:, BLOCK:]], axis=0)

    def work(k, first):
        s = first // GROUPS
        gang = tuple(first + i for i in range(GANG))

        def lanes_of(u, side=0, width=WIDTH):
            return pl.ds(pl.multiple_of((u % GROUPS) * WIDTH + side * width, width), width)

        @pl.when((k == 0) & jnp.logical_not(has_up))
        def _():
            for u in gang:
                flow[0, u] = jnp.zeros(flow.shape[2:], bf16)

        @pl.when(jnp.logical_not(has_left & ((k == 1) | has_up)))
        def _():
            for u in gang:
                edge[k, u] = jnp.zeros(edge.shape[2:], f32)

        @pl.when(jnp.logical_not(has_left))
        def _():
            for u in gang:
                state_in[k, u] = jnp.zeros(state_in.shape[2:], bf16)

        xs_of, falls, locals_one, locals_all, mixed_of = [], [], [], [], []
        for i, u in enumerate(gang):
            gate = (0.5 * gate_buf[k, s, :, lanes_of(u)]).astype(f32)
            opened[i] = silu_of_twice(gate)
        for i, u in enumerate(gang):
            sides = []
            @pl.when((k == 0) & has_up)
            def _(u=u):
                prev_copy(u, 0).wait_recv()

            @pl.when((k == 0) & has_up & has_right)
            def _(u=u):
                edge_out[0, u] = folded(flow[0, u, BLOCK - EDGE :])
                edge_copy(0, u, 1).start()

            @pl.when(has_left & ((k == 1) | has_up))
            def _(u=u):
                edge_copy(k, u).wait_recv()

            for side in range(2):
                at = lanes_of(u, side, BLOCK)
                buf = cbuf.at[2 * i + side]
                buf[pl.ds(0, PAD), :] = heads[k, pl.ds(pl.multiple_of(s * PAD, PAD), PAD), at]
                buf[pl.ds(PAD - KEPT, KEPT), :] += edge[k, u, side * KEPT : (side + 1) * KEPT]
                buf[pl.ds(PAD, BLOCK), :] = x_buf[k, s, :, at].astype(f32) + flow[
                    k, u, :, side * BLOCK : (side + 1) * BLOCK
                ].astype(f32)
                sides.append(conv(buf, w_buf[k, :, at]).astype(bf16))
            xs = jnp.concatenate(sides, axis=1)
            xs_of.append(xs)
            keyed = xs * tails[k, u]
            extra = wides[k, u, BLOCK : BLOCK + PAD]
            fall_one, fall_two = extra[2:3] + extra[3:4], extra[4:5] + extra[5:6]
            local_one = jnp.dot(b_rows[k, u, 0], keyed[:HALF], preferred_element_type=f32)
            local_two = jnp.dot(b_rows[k, u, 1], keyed[HALF:], preferred_element_type=f32)
            falls.append((fall_one, fall_two))
            locals_one.append(local_one)
            locals_all.append(fall_two * local_one + local_two)
        zero = jnp.zeros((HALF, BLOCK), bf16)
        for u, xs in zip(gang, xs_of):
            mixed = []
            for part in range(2):
                tokens = slice(part * HALF, (part + 1) * HALF)
                sides = []
                for side in range(2):
                    xs_side = xs[tokens, side * BLOCK : (side + 1) * BLOCK]
                    diagonal = jnp.concatenate(
                        [jnp.where(lane_head == h, xs_side, zero) for h in range(PER_GROUP // 2)],
                        axis=0,
                    )
                    sides.append(
                        jnp.dot(
                            weights[k, u, tokens, side * WIDTH : (side + 1) * WIDTH],
                            diagonal,
                            preferred_element_type=f32,
                        )
                    )
                mixed.append(jnp.concatenate(sides, axis=1))
            skip = wides[k, u, BLOCK : BLOCK + 1] + wides[k, u, BLOCK + 1 : BLOCK + 2]
            mixed_of.append(jnp.concatenate(mixed, axis=0) + skip * xs.astype(f32))

        arrived = []
        for i, u in enumerate(gang):
            fall_one, fall_two = falls[i]
            fall = fall_one * fall_two
            sides = []

            @pl.when(has_left)
            def _(u=u):
                state_copy(k, u, 0).wait_recv()

            for side in range(2):
                here = slice(side * BLOCK, (side + 1) * BLOCK)
                incoming = state_in[k, u, side].astype(f32)
                state_out[k, u, side] = (fall[:, here] * incoming + locals_all[i][:, here]).astype(
                    bf16
                )
                sides.append(incoming)

            @pl.when(has_right)
            def _(u=u):
                state_copy(k, u).start()

            arrived.append(jnp.concatenate(sides, axis=1))

        for i, u in enumerate(gang):
            incoming = arrived[i]
            between = (falls[i][0] * incoming + locals_one[i]).astype(bf16)
            off = jnp.concatenate(
                [
                    jnp.dot(c_rows[k, u, :HALF], incoming.astype(bf16), preferred_element_type=f32),
                    jnp.dot(c_rows[k, u, HALF:], between, preferred_element_type=f32),
                ],
                axis=0,
            )
            mixed = mixed_of[i] + off * wides[k, u, :BLOCK]
            gated = mixed * opened[i]
            mean = jnp.sum(gated * gated, axis=1, keepdims=True) * (1.0 / WIDTH)
            result = (
                gated * lax.rsqrt(mean + norm_eps) * gain_buf[k, 0:1, lanes_of(u)]
            ).astype(bf16)
            flow[k + 1, u] = result

        @pl.when(has_right & (k == 0))
        def _():
            for u in gang:
                edge_out[1, u] = folded(flow[1, u, BLOCK - EDGE :])
                edge_copy(1, u, 1).start()

        @pl.when((k == 1) & has_down)
        def _():
            for u in gang:
                prev_copy(u).start()

        @pl.when(k == core)
        def _():
            for u in gang:
                out_ref[0, s, :, lanes_of(u)] = flow[k + 1, u]

        @pl.when(k != core)
        def _():
            for u in gang:
                out_copy(k, u).start()

    few, even, all_gangs = FEW // GANG, EVEN // GANG, UNITS // GANG

    def step(i, carry):
        k, i = i % 2, i // 2
        later = jnp.maximum(i - few, 0)
        u = GANG * jnp.where(
            core == 0,
            i,
            jnp.where(i < few, even + i, few + later // 2 + even * (1 - later % 2)),
        )
        p = u // 2

        @pl.when((u >= low) & (u < low + many))
        def _():
            @pl.when(first_chip & ((k != core) | ((core == 0) & (p >= 2))) & (u % 2 == 0))
            def _():
                prepare(k, p)

            @pl.when((k != core) & (u % 2 == 0))
            def _():
                swap_wait(1, k, p)

            work(k, u)

        return carry

    lax.fori_loop(0, 2 * (even + core * (all_gangs - even - few)), step, 0)

    for i in range(5):
        part_copy(i, core).wait_send()

    @pl.when(has_right)
    def _():
        for i in range(3):
            head_copy(core, i).wait_send()

    def sent(ref, send, there):
        @pl.when(there)
        def _():
            remote(ref, ref, send, out_recv, other).wait_send()

    for n in sorted({FEW // 2, EVEN // 2, PAIRS - FEW // 2}):
        sent(flow.at[0, pl.ds(0, n)], swap_send.at[0], far_pairs == n)
        sent(flow.at[pl.ds(0, 2), pl.ds(0, 2 * n)], swap_send.at[1], far_pairs == n)
        these = n_pairs == n
        sent(state_out.at[:, pl.ds(0, 2 * n)], state_send, these & has_right)
        sent(edge_out.at[1, pl.ds(0, 2 * n)], edge_send.at[1], these & has_right)
        sent(edge_out.at[0, pl.ds(0, 2 * n)], edge_send.at[0], these & has_right & has_up)
        sent(flow.at[0, pl.ds(0, 2 * n)], prev_send, these & has_down)
        sent(flow.at[0, pl.ds(0, 2 * n)], out_send, these)

        @pl.when(far_pairs == n)
        def _(n=n):
            ref = flow.at[0, pl.ds(0, 2 * n)]
            remote(ref, ref, out_send, out_recv, other).wait_recv()


def solution(mesh):
    stages, ranges = mesh.shape["pipe"] // 2, mesh.shape["ctx"]
    f32, bf16 = jnp.float32, jnp.bfloat16
    vmem = pl.BlockSpec(memory_space=pltpu.VMEM)
    hbm = pl.BlockSpec(memory_space=pltpu.HBM)
    dma = pltpu.SemaphoreType.DMA
    pin = functools.partial(pltpu.with_memory_space_constraint, memory_space=pltpu.HBM)

    def on_device(x, gate, bc, dt, rate, weight, skip, gain):
        channels = x.shape[3] + bc.shape[3]
        return pl.pallas_call(
            functools.partial(kernel, stages, ranges),
            out_shape=jax.ShapeDtypeStruct(x.shape, bf16),
            in_specs=[hbm] * 8,
            out_specs=vmem,
            scratch_shapes=[
                pltpu.VMEM((1, SEQS, HEADS, BLOCK), f32),
                pltpu.VMEM(rate.shape, f32),
                pltpu.VMEM(skip.shape, f32),
                pltpu.VMEM((2,) + weight.shape[1:], f32),
                pltpu.VMEM((2,) + gain.shape, f32),
                pltpu.VMEM((2,) + x.shape[1:], bf16),
                pltpu.VMEM((2,) + gate.shape[1:], bf16),
                pltpu.VMEM((2,) + bc.shape[1:], bf16),
                pltpu.VMEM((2, UNITS // 4, BLOCK, BLOCK), bf16),
                pltpu.VMEM((2, BLOCK, PER_GROUP * HALF), bf16),
                pltpu.VMEM((2, ROWS, BLOCK), bf16),
                pltpu.VMEM((BLOCK, BLOCK), f32),
                pltpu.VMEM((3 * 32, PER_GROUP * HALF), bf16),
                pltpu.VMEM((HALF, PER_GROUP * HALF), bf16),
                pltpu.VMEM((2 * BLOCK, 2 * WIDTH), bf16),
                pltpu.VMEM((2, UNITS, BLOCK, PER_GROUP * HALF), bf16),
                pltpu.VMEM((2, UNITS, 2, STATE, HALF), bf16),
                pltpu.VMEM((2, UNITS, BLOCK, STATE), bf16),
                pltpu.VMEM((2, UNITS, BLOCK + EDGE, WIDTH), f32),
                pltpu.VMEM((2, UNITS, BLOCK, WIDTH), bf16),
                pltpu.VMEM((GANG, BLOCK, WIDTH), f32),
                pltpu.VMEM((2 * GANG, PAD + BLOCK, BLOCK), f32),
                pltpu.VMEM((2, PAD + BLOCK, 2 * STATE), f32),
                pltpu.VMEM((SEQS, EDGE, FOLD), bf16),
                pltpu.VMEM((2, SEQS, EDGE, FOLD), bf16),
                pltpu.VMEM((2, SEQS * PAD, channels), f32),
                pltpu.VMEM((3, UNITS, BLOCK, WIDTH), bf16),
                pltpu.VMEM((2, UNITS, PAD, BLOCK), f32),
                pltpu.VMEM((2, UNITS, PAD, BLOCK), f32),
                pltpu.VMEM((2, UNITS, 2, STATE, BLOCK), bf16),
                pltpu.VMEM((2, UNITS, 2, STATE, BLOCK), bf16),
                dma((8,)),
                dma((5,)),
                dma((5,)),
                dma((2,)),
                dma((2, MOST // 2)),
                dma((3,)),
                dma((2, SEQS)),
                dma(()),
                dma((MOST,)),
                dma((2,)),
                dma((2, MOST)),
                dma(()),
                dma((2, MOST)),
                dma(()),
                dma(()),
            ],
            compiler_params=pltpu.CompilerParams(
                collective_id=0, has_side_effects=True, vmem_limit_bytes=52 * 1024 * 1024
            ),
            name="relay",
        )(*map(pin, (x, gate, bc, jnp.swapaxes(dt, 2, 3), rate, weight, skip, gain)))

    rows = P("pipe", None, "ctx", None)
    in_specs = (rows, rows, rows, rows, P("pipe", None), P("pipe", None, None), P("pipe", None), P("pipe", None))
    return jax.shard_map(on_device, mesh=mesh, in_specs=in_specs, out_specs=rows, check_vma=False)
```
